256 devices in a mesh: group: 4 (over y), dom: 64 (over z, x, core).
Axes of the slice: x: 4, y: 4, z: 8, core: 2. Of those that a mesh axis runs over, the one named last changes fastest.
Arguments:
- node_lat: bfloat16 [524288, 256], P(('group', 'dom')), may hold values from -6 to 6
- edge_lat: bfloat16 [2097152, 256], P(('group', 'dom')), may hold values from -6 to 6
- edge_send: int32 [2097152], P(('group', 'dom')), may hold values from 0 to 3071, as said below
- halo_list: int32 [262144], P(('group', 'dom')), may hold values from 0 to 2047
- pool_id: int32 [524288], P(('group', 'dom')), may hold values from 0 to 1023
- coarse_lat: bfloat16 [65536, 256], P(('group', 'dom')), may hold values from -6 to 6
- cedge_lat: bfloat16 [262144, 256], P(('group', 'dom')), may hold values from -6 to 6
- cedge_send: int32 [262144], P(('group', 'dom')), may hold values from 0 to 511, as said below
- chalo_list: int32 [65536], P(('group', 'dom')), may hold values from 0 to 255
- fine_edge_in: bfloat16 [3, 256, 256], replicated, may hold values from -0.21875 to 0.21875
- fine_edge_out: bfloat16 [256, 256], replicated, may hold values from -0.375 to 0.375
- fine_node_in: bfloat16 [2, 256, 256], replicated, may hold values from -0.25 to 0.25
- fine_node_out: bfloat16 [256, 256], replicated, may hold values from -0.375 to 0.375
- fine_bias: float32 [4, 256], replicated, may hold values from -3 to 3
- fine_gain: float32 [2, 256], replicated, may hold values from 0.1 to 1.9
- coarse_edge_in: bfloat16 [3, 256, 256], replicated, may hold values from -0.21875 to 0.21875
- coarse_edge_out: bfloat16 [256, 256], replicated, may hold values from -0.375 to 0.375
- coarse_node_in: bfloat16 [2, 256, 256], replicated, may hold values from -0.25 to 0.25
- coarse_node_out: bfloat16 [256, 256], replicated, may hold values from -0.375 to 0.375
- coarse_bias: float32 [4, 256], replicated, may hold values from -3 to 3
- coarse_gain: float32 [2, 256], replicated, may hold values from 0.1 to 1.9
Outputs:
- fine_out: bfloat16 [524288, 256], P(('group', 'dom'))
- coarse_out: bfloat16 [65536, 256], P(('group', 'dom'))
The draws below stay inside these ranges and needn't reach their ends.
Inputs may be any that keep to these rules, and one draw needn't show every extreme that they name: `edge_send`: indices into the block's extended rows: below 512 the lower neighbour's rows, from 2560 on the upper neighbour's; a block never names the rows of a neighbour it lacks. `cedge_send`: indices into the block's extended coarse rows: below 128 the lower neighbour's rows, from 384 on the upper neighbour's; a block never names the rows of a neighbour it lacks.
All inputs are finite; a program needn't handle non-finite values.
Results may differ from the reference program's by a relative error of at most 0.012.
Values may be sent and summed in bfloat16 or wider, within the bound.
No kernel may reach another device: no remote copies, remote signals or barrier semaphores. Data moves between devices by JAX's collectives and lax.ppermute only.
A program may use at most 128 MiB of HBM per device.

```python
import math
import jax
import jax.numpy as jnp
import numpy as np
from jax import lax

H = 256
DEG = 4
NODE_DEV = 2048
EDGE_DEV = 8192
HALO = 512
CDEV = 256
CHALO = 128
CEDGE_DEV = 1024
CLUSTERS_COL = 1024
NODES = 524288
EDGES = 2097152
CNODES = 65536
CEDGES = 262144
N_GROUP = 4
N_DOM = 64


def rim_senders(base_key, count_all, per_block, row_count, rim_rows, across_odds):
    blocks = jnp.arange(count_all) // per_block % N_DOM
    key_own, key_side, key_place, key_across = jax.random.split(base_key, 4)
    own_index = rim_rows + jax.random.randint(key_own, (count_all,), 0, row_count)
    which_side = jax.random.randint(key_side, (count_all,), 0, 2)
    which_side = jnp.where(blocks == 0, 1, jnp.where(blocks == N_DOM - 1, 0, which_side))
    rim_place = jax.random.randint(key_place, (count_all,), 0, rim_rows)
    remote = jnp.where(which_side == 0, rim_place, rim_rows + row_count + rim_place)
    across = jax.random.randint(key_across, (count_all,), 0, across_odds) == 0
    return jnp.where(across, remote, own_index).astype(jnp.int32)


def draw_edge_send(key, part):
    return rim_senders(jax.random.fold_in(key, 5), EDGES, EDGE_DEV, NODE_DEV, HALO, 8)


def draw_cedge_send(key, part):
    return rim_senders(jax.random.fold_in(key, 7), CEDGES, CEDGE_DEV, CDEV, CHALO, 2)


def touch_ends(drawn, rng, low, high):
    extent = drawn.shape
    index_at = [jax.random.randint(jax.random.fold_in(rng, axis), (), 0, extent[axis]) for axis in range(len(extent))]
    drawn = drawn.at[tuple(index_at)].set(low)
    longest = extent.index(max(extent))
    index_at[longest] = (index_at[longest] + 1) % extent[longest]
    return drawn.at[tuple(index_at)].set(high)


def steps_of(own_key, dims, cuts, least, high):
    def one(dim, blocks):
        heights = jax.random.uniform(jax.random.fold_in(jax.random.fold_in(own_key, 6), dim), (blocks,), jnp.float32, least / len(cuts), high / len(cuts))
        return jnp.repeat(jnp.exp(heights), dims[dim] // blocks).reshape((-1,) + (1,) * (len(dims) - dim - 1))

    loudness = one(*cuts[0])
    for cut in cuts[1:]:
        loudness = loudness * one(*cut)
    return loudness


def rank_bounds(number_of, skew):
    portions = [(1 << 20) // math.isqrt(rank ** skew) + 1 for rank in range(1, number_of + 1)]
    scale = 1 + sum(portions) // (1 << 30)
    return np.cumsum(np.array([max(1, weight // scale) for weight in portions]))


def ranked_ids(own_key, extent, number_of, skew):
    grid = rank_bounds(number_of, skew)
    ticket = jax.random.randint(jax.random.fold_in(own_key, 1), extent, 0, int(grid[number_of - 1]))
    rank = jnp.searchsorted(jnp.asarray(grid, jnp.int32), ticket, side="right")
    return jax.random.permutation(jax.random.fold_in(own_key, 2), number_of)[rank].astype(jnp.int32)


def gaussian(stream_key, extent, spread, reach, cuts=(), kind=jnp.bfloat16):
    factor_of = steps_of(stream_key, extent, cuts, -0.22, 0.18) if cuts else 1.0
    array = jax.random.normal(stream_key, extent, jnp.float32) * spread * factor_of
    return jnp.minimum(jnp.maximum(array, -reach), reach).astype(kind)


def setup_inputs(seed: int = 0) -> dict:
    arg_keys = jax.random.split(jax.random.key(seed), 22)
    return {
        "node_lat": gaussian(arg_keys[0], (NODES, H), 1.0, 6.0, ((0, 256),)),
        "edge_lat": gaussian(arg_keys[1], (EDGES, H), 1.0, 6.0, ((0, 256),)),
        "edge_send": draw_edge_send(jax.random.fold_in(arg_keys[21], 71), 0),
        "halo_list": touch_ends(jax.random.randint(arg_keys[3], (N_GROUP * N_DOM * 2 * HALO,), 0, NODE_DEV), jax.random.fold_in(arg_keys[3], 1), 0, NODE_DEV - 1).astype(jnp.int32),
        "pool_id": touch_ends(ranked_ids(arg_keys[4], (NODES,), CLUSTERS_COL, 1), jax.random.fold_in(arg_keys[4], 3), 0, CLUSTERS_COL - 1).astype(jnp.int32),
        "coarse_lat": gaussian(arg_keys[5], (CNODES, H), 1.0, 6.0, ((0, 256),)),
        "cedge_lat": gaussian(arg_keys[6], (CEDGES, H), 1.0, 6.0, ((0, 256),)),
        "cedge_send": draw_cedge_send(jax.random.fold_in(arg_keys[21], 71), 0),
        "chalo_list": touch_ends(jax.random.randint(arg_keys[8], (N_GROUP * N_DOM * 2 * CHALO,), 0, CDEV), jax.random.fold_in(arg_keys[8], 1), 0, CDEV - 1).astype(jnp.int32),
        "fine_edge_in": gaussian(arg_keys[9], (3, H, H), (3 * H) ** -0.5, 0.21875),
        "fine_edge_out": gaussian(arg_keys[10], (H, H), H ** -0.5, 0.375),
        "fine_node_in": gaussian(arg_keys[11], (2, H, H), (2 * H) ** -0.5, 0.25),
        "fine_node_out": gaussian(arg_keys[12], (H, H), H ** -0.5, 0.375),
        "fine_bias": gaussian(arg_keys[13], (4, H), 0.5, 3.0, (), jnp.float32),
        "fine_gain": jnp.clip(1.0 + 0.18 * jax.random.normal(arg_keys[14], (2, H), jnp.float32), 0.1, 1.9),
        "coarse_edge_in": gaussian(arg_keys[15], (3, H, H), (3 * H) ** -0.5, 0.21875),
        "coarse_edge_out": gaussian(arg_keys[16], (H, H), H ** -0.5, 0.375),
        "coarse_node_in": gaussian(arg_keys[17], (2, H, H), (2 * H) ** -0.5, 0.25),
        "coarse_node_out": gaussian(arg_keys[18], (H, H), H ** -0.5, 0.375),
        "coarse_bias": gaussian(arg_keys[19], (4, H), 0.5, 3.0, (), jnp.float32),
        "coarse_gain": jnp.clip(1.0 + 0.18 * jax.random.normal(arg_keys[20], (2, H), jnp.float32), 0.1, 1.9),
    }


EPSILON = 1e-05

def layer_norm_rows(values):
    row_mean = lax.optimization_barrier(jnp.mean(values, axis=-1, keepdims=True))
    centred = values - row_mean
    variance = lax.optimization_barrier(jnp.mean(centred * centred, axis=-1, keepdims=True))
    return centred * lax.rsqrt(variance + EPSILON)

def edge_node(sender_proj, own_rows, edge_rows, senders, edge_in, edge_out, node_in, node_out, biases, gains):
    node_count = own_rows.shape[0]
    width = own_rows.shape[1]
    receiver_proj = jnp.dot(own_rows, edge_in[1], preferred_element_type=jnp.float32)
    edge_pre = jnp.dot(edge_rows, edge_in[2], preferred_element_type=jnp.float32)
    edge_pre = edge_pre + sender_proj[senders].astype(jnp.float32) + biases[0]
    edge_pre = (edge_pre.reshape(node_count, DEG, width) + receiver_proj[:, None, :]).reshape(node_count * DEG, width)
    edge_hidden = jnp.maximum(edge_pre, 0.0).astype(jnp.bfloat16)
    message = layer_norm_rows(jnp.dot(edge_hidden, edge_out, preferred_element_type=jnp.float32) + biases[1]) * gains[0]
    message = message.astype(jnp.bfloat16)
    summed = lax.optimization_barrier(jnp.sum(message.astype(jnp.float32).reshape(node_count, DEG, width), axis=1)).astype(jnp.bfloat16)
    node_pre = jnp.dot(own_rows, node_in[0], preferred_element_type=jnp.float32)
    node_pre = node_pre + jnp.dot(summed, node_in[1], preferred_element_type=jnp.float32) + biases[2]
    node_hidden = jnp.maximum(node_pre, 0.0).astype(jnp.bfloat16)
    update = layer_norm_rows(jnp.dot(node_hidden, node_out, preferred_element_type=jnp.float32) + biases[3]) * gains[1]
    return (own_rows.astype(jnp.float32) + update).astype(jnp.bfloat16)

def pick_rows(block_rows, chosen):
    return block_rows[chosen]

def extend_blocks(blocks, lists, rim_rows):
    border = jax.vmap(jax.vmap(pick_rows))(blocks, lists)
    zeros_rim = jnp.zeros_like(border[:, :1, :rim_rows])
    from_lower = jnp.concatenate([zeros_rim, border[:, :-1, rim_rows:]], axis=1)
    from_upper = jnp.concatenate([border[:, 1:, :rim_rows], zeros_rim], axis=1)
    return jnp.concatenate([from_lower, blocks, from_upper], axis=2)

def run_level(node_rows, edge_rows, senders, lists, per_nodes, per_edges, rim_rows, edge_in, edge_out, node_in, node_out, biases, gains):
    block_count = N_GROUP * N_DOM
    width = node_rows.shape[1]
    blocks = node_rows.reshape(N_GROUP, N_DOM, per_nodes, width)
    chosen = lists.reshape(N_GROUP, N_DOM, 2 * rim_rows)
    extended = extend_blocks(blocks, chosen, rim_rows).reshape(block_count, per_nodes + 2 * rim_rows, width)

    def one_block(pieces):
        ext_rows, own_rows, block_edges, send_idx = pieces
        sender_proj = jnp.dot(ext_rows, edge_in[0], preferred_element_type=jnp.float32).astype(jnp.bfloat16)
        return edge_node(sender_proj, own_rows, block_edges, send_idx, edge_in, edge_out, node_in, node_out, biases, gains)
    result = lax.map(one_block, (extended, node_rows.reshape(block_count, per_nodes, width), edge_rows.reshape(block_count, per_edges, width), senders.reshape(block_count, per_edges)))
    return result.reshape(block_count * per_nodes, width)

def reference(node_lat, edge_lat, edge_send, halo_list, pool_id, coarse_lat, cedge_lat, cedge_send, chalo_list, fine_edge_in, fine_edge_out, fine_node_in, fine_node_out, fine_bias, fine_gain, coarse_edge_in, coarse_edge_out, coarse_node_in, coarse_node_out, coarse_bias, coarse_gain):
    block_count = N_GROUP * N_DOM
    fine_out = run_level(node_lat, edge_lat, edge_send, halo_list, NODE_DEV, EDGE_DEV, HALO, fine_edge_in, fine_edge_out, fine_node_in, fine_node_out, fine_bias, fine_gain)

    def block_pool(pieces):
        block_rows, block_ids = pieces
        cluster_sum = jax.ops.segment_sum(block_rows.astype(jnp.float32), block_ids, num_segments=CLUSTERS_COL)
        member_count = jax.ops.segment_sum(jnp.ones(block_ids.shape, jnp.float32), block_ids, num_segments=CLUSTERS_COL)
        return (cluster_sum, member_count)
    partial_sums, partial_counts = lax.map(block_pool, (fine_out.reshape(block_count, NODE_DEV, H), pool_id.reshape(block_count, NODE_DEV)))
    cluster_sum = partial_sums.reshape(N_GROUP, N_DOM, N_GROUP, CDEV, H).sum(axis=0).transpose(1, 0, 2, 3)
    member_count = partial_counts.reshape(N_GROUP, N_DOM, N_GROUP, CDEV).sum(axis=0).transpose(1, 0, 2)
    pooled_mean = cluster_sum / jnp.maximum(member_count, 1.0)[..., None]
    coarse_in = (coarse_lat.astype(jnp.float32) + pooled_mean.reshape(CNODES, H)).astype(jnp.bfloat16)
    coarse_out = run_level(coarse_in, cedge_lat, cedge_send, chalo_list, CDEV, CEDGE_DEV, CHALO, coarse_edge_in, coarse_edge_out, coarse_node_in, coarse_node_out, coarse_bias, coarse_gain)
    return (fine_out, coarse_out)
```

```python
import jax
import jax.numpy as jnp
from jax import lax
from jax.experimental import pallas as pl
from jax.experimental.pallas import tpu as pltpu
from jax.sharding import PartitionSpec as P

EPSILON = 1e-05
F32 = jnp.float32
BF16 = jnp.bfloat16
CHUNK = 1024
TILE = 256
DEG = 4

VMEM_SPEC = pl.BlockSpec(memory_space=pltpu.VMEM)
ANY_SPEC = pl.BlockSpec(memory_space=pl.ANY)


def dot(a, b):
    return jnp.dot(a, b, preferred_element_type=F32)


def centred_weight(w):
    w = w.astype(F32)
    return (w - jnp.mean(w, axis=-1, keepdims=True)).astype(BF16)


def centred_row(b):
    return b - jnp.mean(b, axis=-1, keepdims=True)


def scaled_rows(z):
    mean_square = jnp.mean(z * z, axis=-1, keepdims=True)
    return z * lax.rsqrt(mean_square + EPSILON)


def store_split(table, row, values):
    n = values.shape[0]
    table[pl.ds(2 * row, n, stride=2), :] = values[:, :128]
    table[pl.ds(2 * row + 1, n, stride=2), :] = values[:, 128:]


def load_split(table, row, n):
    return jnp.concatenate(
        [table[pl.ds(2 * row, n, stride=2), :], table[pl.ds(2 * row + 1, n, stride=2), :]],
        axis=1,
    )


def border_kernel(list_ref, node_ref, w_ref, a_ref, b_ref, table, rows, index, sem):
    rim = a_ref.shape[0]
    odd = lax.rem(lax.axis_index("dom"), 2)
    first = pl.multiple_of((1 - odd) * rim, rim)
    second = pl.multiple_of(odd * rim, rim)
    copies = [
        pltpu.make_async_copy(list_ref.at[pl.ds(first, rim)], index.at[pl.ds(0, rim)], sem.at[0]),
        pltpu.make_async_copy(
            list_ref.at[pl.ds(second, rim)], index.at[pl.ds(rim, rim)], sem.at[1]
        ),
    ]
    for c in copies:
        c.start()
    w = w_ref[0]
    for i in range(node_ref.shape[0] // TILE):
        p = dot(node_ref[i * TILE : (i + 1) * TILE, :], w)
        store_split(table, i * TILE, p.astype(BF16).astype(F32))
    for c in copies:
        c.wait()
    for part, out in enumerate((a_ref, b_ref)):
        for u in range(rim):
            at = part * rim + u
            row = pl.multiple_of(index[at] * 2, 2)
            rows[pl.ds(2 * at, 2), :] = table[pl.ds(row, 2), :]
        for i in range(0, rim, TILE):
            out[i : i + TILE, :] = load_split(rows, part * rim + i, TILE).astype(BF16)


def border_rows(lists, nodes, edge_in, rim):
    shape = jax.ShapeDtypeStruct((rim, 256), BF16)
    return pl.pallas_call(
        border_kernel,
        out_shape=(shape, shape),
        in_specs=[ANY_SPEC, VMEM_SPEC, VMEM_SPEC],
        out_specs=(VMEM_SPEC, VMEM_SPEC),
        scratch_shapes=[
            pltpu.VMEM((2 * nodes.shape[0], 128), F32),
            pltpu.VMEM((4 * rim, 128), F32),
            pltpu.SMEM((2 * rim,), jnp.int32),
            pltpu.SemaphoreType.DMA((2,)),
        ],
        cost_estimate=pl.CostEstimate(flops=300_000_000, bytes_accessed=2_000_000, transcendentals=0),
        name="border_rows",
    )(lists, nodes, edge_in)


def fine_kernel(
    send_ref,
    edge_ref,
    node_ref,
    low_ref,
    high_ref,
    pool_ref,
    edge_in,
    edge_out,
    node_in,
    node_out,
    bias,
    gain,
    out_ref,
    pooled_ref,
    table,
    edges,
    rows0,
    rows1,
    index0,
    index1,
    w_edge,
    w_node,
    edge_sem,
    index_sem,
):
    nodes = node_ref.shape[0]
    chunks = edges.shape[0] // CHUNK
    rim = low_ref.shape[0]
    cnodes = CHUNK // DEG

    def edge_copy(c):
        at = pl.ds(pl.multiple_of(c * CHUNK, CHUNK), CHUNK)
        return pltpu.make_async_copy(edge_ref.at[at, :], edges.at[at, :], edge_sem.at[c])

    def index_copy(c, index, slot):
        at = pl.ds(pl.multiple_of(c * CHUNK, CHUNK), CHUNK)
        return pltpu.make_async_copy(send_ref.at[at], index, index_sem.at[slot])

    index_copy(0, index0, 0).start()
    index_copy(1, index1, 1).start()
    for c in range(chunks):
        edge_copy(c).start()

    w = edge_in[0]
    for i in range(nodes // TILE):
        p = dot(node_ref[i * TILE : (i + 1) * TILE, :], w)
        store_split(table, i * TILE, p.astype(BF16).astype(F32))
    for i in range(0, rim, TILE):
        store_split(table, nodes + i, low_ref[i : i + TILE, :].astype(F32))
        store_split(table, nodes + rim + i, high_ref[i : i + TILE, :].astype(F32))
    w_edge[...] = centred_weight(edge_out[...])
    w_node[...] = centred_weight(node_out[...])
    b_edge = bias[0:1, :]
    b_message = centred_row(bias[1:2, :])
    b_node = bias[2:3, :]
    b_update = centred_row(bias[3:4, :])
    g_message = gain[0:1, :]
    g_update = gain[1:2, :]
    tnodes = TILE // DEG
    spread = (
        lax.broadcasted_iota(jnp.int32, (TILE, tnodes), 0) // DEG
        == lax.broadcasted_iota(jnp.int32, (TILE, tnodes), 1)
    ).astype(F32).astype(BF16)
    collect = (
        lax.broadcasted_iota(jnp.int32, (tnodes, TILE), 1) // DEG
        == lax.broadcasted_iota(jnp.int32, (tnodes, TILE), 0)
    ).astype(F32).astype(BF16)

    def gather(index, rows, start, count):
        for u in range(start, start + count):
            row = pl.multiple_of(index[u], 2)
            rows[2 * u : 2 * u + 2, :] = table[pl.ds(row, 2), :]

    def compute(c, rows, fetch):
        edge_copy(c).wait()
        own = node_ref[pl.ds(pl.multiple_of(c * cnodes, cnodes), cnodes), :]
        receiver = (dot(own, edge_in[1]) + b_edge).astype(BF16)
        sums = []
        tiles = CHUNK // TILE
        for t in range(tiles):
            x = edges[pl.ds(pl.multiple_of(c * CHUNK + t * TILE, TILE), TILE), :]
            pre = dot(x, edge_in[2]) + dot(spread, receiver[t * tnodes : (t + 1) * tnodes, :])
            pre = pre + load_split(rows, t * TILE, TILE)
            hidden = jnp.maximum(pre, 0.0).astype(BF16)
            z = dot(hidden, w_edge[...]) + b_message
            sums.append(dot(collect, scaled_rows(z).astype(BF16)))
            fetch(t * TILE, TILE)
        summed = (jnp.concatenate(sums, axis=0) * g_message).astype(BF16)
        pre = dot(own, node_in[0]) + dot(summed, node_in[1]) + b_node
        hidden = jnp.maximum(pre, 0.0).astype(BF16)
        u = scaled_rows(dot(hidden, w_node[...]) + b_update) * g_update
        out_ref[pl.ds(pl.multiple_of(c * cnodes, cnodes), cnodes), :] = (
            own.astype(F32) + u
        ).astype(BF16)

    index_copy(0, index0, 0).wait()
    gather(index0, rows0, 0, CHUNK)
    index_copy(2, index0, 0).start()

    def pair(k, carry):
        c = 2 * k
        index_copy(c + 1, index1, 1).wait()
        compute(c, rows0, lambda s, n: gather(index1, rows1, s, n))
        index_copy(jnp.minimum(c + 3, chunks - 1), index1, 1).start()
        index_copy(jnp.minimum(c + 2, chunks - 1), index0, 0).wait()
        compute(c + 1, rows1, lambda s, n: gather(index0, rows0, s, n))
        index_copy(jnp.minimum(c + 4, chunks - 1), index0, 0).start()
        return carry

    lax.fori_loop(0, chunks // 2, pair, 0)
    index_copy(0, index0, 0).wait()
    index_copy(1, index1, 1).wait()

    ids = pool_ref[...]
    owners = pooled_ref.shape[0]
    cluster_rows = 256
    for g in range(owners):
        member = (
            lax.broadcasted_iota(jnp.int32, (cluster_rows, nodes), 0) + g * cluster_rows == ids
        ).astype(F32)
        pooled_ref[g, :cluster_rows, :] = dot(member.astype(BF16), out_ref[...]).astype(BF16)
        count = jnp.sum(member, axis=1, keepdims=True)
        high = jnp.floor(count * (1.0 / 256.0))
        low = count - high * 256.0
        both = jnp.where(
            lax.broadcasted_iota(jnp.int32, (cluster_rows, 128), 1) == 0,
            low,
            jnp.where(lax.broadcasted_iota(jnp.int32, (cluster_rows, 128), 1) == 1, high, 0.0),
        )
        flipped = both.T[:16, :]
        pooled_ref[g, cluster_rows:, :] = flipped.astype(BF16)


def fine_level(send, edges, nodes, low, high, pool, edge_in, edge_out, node_in, node_out, bias, gain, owners):
    n = nodes.shape[0]
    rim = low.shape[0]
    return pl.pallas_call(
        fine_kernel,
        out_shape=(
            jax.ShapeDtypeStruct((n, 256), BF16),
            jax.ShapeDtypeStruct((owners, 272, 256), BF16),
        ),
        in_specs=[ANY_SPEC, ANY_SPEC] + [VMEM_SPEC] * 10,
        out_specs=(VMEM_SPEC, VMEM_SPEC),
        scratch_shapes=[
            pltpu.VMEM((2 * (n + 2 * rim), 128), F32),
            pltpu.VMEM(edges.shape, BF16),
            pltpu.VMEM((2 * CHUNK, 128), F32),
            pltpu.VMEM((2 * CHUNK, 128), F32),
            pltpu.SMEM((CHUNK,), jnp.int32),
            pltpu.SMEM((CHUNK,), jnp.int32),
            pltpu.VMEM((256, 256), BF16),
            pltpu.VMEM((256, 256), BF16),
            pltpu.SemaphoreType.DMA((edges.shape[0] // CHUNK,)),
            pltpu.SemaphoreType.DMA((2,)),
        ],
        cost_estimate=pl.CostEstimate(flops=6_000_000_000, bytes_accessed=8_000_000, transcendentals=0),
        name="fine_level",
    )(send, edges, nodes, low, high, pool, edge_in, edge_out, node_in, node_out, bias, gain)


def one_hot_rows(index_col, count):
    return (
        index_col == lax.broadcasted_iota(jnp.int32, (index_col.shape[0], count), 1)
    ).astype(F32).astype(BF16)


def cluster_kernel(parts_ref, lat_ref, list_ref, w_ref, in_ref, proj_ref, border_ref):
    clusters = lat_ref.shape[0]
    total = parts_ref[0, :clusters, :].astype(F32)
    tail = parts_ref[0, clusters:, :].astype(F32)
    for g in range(1, parts_ref.shape[0]):
        total = total + parts_ref[g, :clusters, :].astype(F32)
        tail = tail + parts_ref[g, clusters:, :].astype(F32)
    count = tail[0:1, :] + 256.0 * tail[1:2, :]
    count = jnp.broadcast_to(count, (8, clusters)).T[:, :1]
    mean = total / jnp.maximum(count, 1.0)
    coarse_in = (lat_ref[...].astype(F32) + mean).astype(BF16)
    in_ref[...] = coarse_in
    proj = dot(coarse_in, w_ref[0]).astype(BF16)
    proj_ref[...] = proj
    picked = one_hot_rows(list_ref[...], clusters)
    border_ref[...] = dot(picked, proj).astype(BF16)


def cluster_level(parts, lat, lists, edge_in):
    n = lat.shape[0]
    shape = jax.ShapeDtypeStruct((n, 256), BF16)
    return pl.pallas_call(
        cluster_kernel,
        out_shape=(shape, shape, jax.ShapeDtypeStruct((lists.shape[0], 256), BF16)),
        in_specs=[VMEM_SPEC] * 4,
        out_specs=(VMEM_SPEC,) * 3,
        cost_estimate=pl.CostEstimate(flops=70_000_000, bytes_accessed=1_000_000, transcendentals=0),
        name="cluster_level",
    )(parts, lat, lists, edge_in)


def coarse_kernel(
    send_ref, edge_ref, node_ref, proj_ref, low_ref, high_ref, edge_in, edge_out, node_in, node_out, bias, gain, out_ref
):
    nodes = node_ref.shape[0]
    rim = low_ref.shape[0]
    count = edge_ref.shape[0]
    table = jnp.concatenate([proj_ref[...], low_ref[...], high_ref[...]], axis=0)
    w_edge = centred_weight(edge_out[...])
    w_node = centred_weight(node_out[...])
    b_message = centred_row(bias[1:2, :])
    b_update = centred_row(bias[3:4, :])
    tnodes = TILE // DEG
    spread = (
        lax.broadcasted_iota(jnp.int32, (TILE, tnodes), 0) // DEG
        == lax.broadcasted_iota(jnp.int32, (TILE, tnodes), 1)
    ).astype(F32).astype(BF16)
    collect = (
        lax.broadcasted_iota(jnp.int32, (tnodes, TILE), 1) // DEG
        == lax.broadcasted_iota(jnp.int32, (tnodes, TILE), 0)
    ).astype(F32).astype(BF16)
    own = node_ref[...]
    receiver = (dot(own, edge_in[1]) + bias[0:1, :]).astype(BF16)
    sums = []
    for t in range(count // TILE):
        x = edge_ref[t * TILE : (t + 1) * TILE, :]
        picked = one_hot_rows(send_ref[t * TILE : (t + 1) * TILE, :], nodes + 2 * rim)
        pre = dot(x, edge_in[2]) + dot(spread, receiver[t * tnodes : (t + 1) * tnodes, :])
        pre = pre + dot(picked, table)
        hidden = jnp.maximum(pre, 0.0).astype(BF16)
        z = dot(hidden, w_edge) + b_message
        sums.append(dot(collect, scaled_rows(z).astype(BF16)))
    summed = (jnp.concatenate(sums, axis=0) * gain[0:1, :]).astype(BF16)
    pre = dot(own, node_in[0]) + dot(summed, node_in[1]) + bias[2:3, :]
    hidden = jnp.maximum(pre, 0.0).astype(BF16)
    u = scaled_rows(dot(hidden, w_node) + b_update) * gain[1:2, :]
    out_ref[...] = (own.astype(F32) + u).astype(BF16)


def coarse_level(send, edges, nodes, proj, low, high, edge_in, edge_out, node_in, node_out, bias, gain):
    return pl.pallas_call(
        coarse_kernel,
        out_shape=jax.ShapeDtypeStruct(nodes.shape, BF16),
        in_specs=[VMEM_SPEC] * 12,
        out_specs=VMEM_SPEC,
        cost_estimate=pl.CostEstimate(flops=800_000_000, bytes_accessed=3_000_000, transcendentals=0),
        name="coarse_level",
    )(send, edges, nodes, proj, low, high, edge_in, edge_out, node_in, node_out, bias, gain)


def pair_swaps():
    count = lax.axis_size("dom")
    inner = [(i, i ^ 1) for i in range(count)]
    outer = [(i, ((i + 1) ^ 1) - 1) for i in range(1, count - 1)]
    return inner, outer


def body(
    node_lat,
    edge_lat,
    edge_send,
    halo_list,
    pool_id,
    coarse_lat,
    cedge_lat,
    cedge_send,
    chalo_list,
    fine_edge_in,
    fine_edge_out,
    fine_node_in,
    fine_node_out,
    fine_bias,
    fine_gain,
    coarse_edge_in,
    coarse_edge_out,
    coarse_node_in,
    coarse_node_out,
    coarse_bias,
    coarse_gain,
):
    inner, outer = pair_swaps()
    odd = lax.rem(lax.axis_index("dom"), 2)
    rim = halo_list.shape[0] // 2
    nodes = node_lat.shape[0]

    def table_row(send, count, rim_rows):
        lower = jnp.where(odd == 1, count, count + rim_rows)
        upper = jnp.where(odd == 1, count + rim_rows, count)
        return jnp.where(
            send < rim_rows,
            send + lower,
            jnp.where(
                send < rim_rows + count, send - rim_rows, send - (rim_rows + count) + upper
            ),
        )

    border_a, border_b = border_rows(halo_list, node_lat, fine_edge_in, rim)
    rim_a = lax.ppermute(border_a, "dom", inner)
    rim_b = lax.ppermute(border_b, "dom", outer)
    send = table_row(edge_send, nodes, rim) * 2
    groups = lax.axis_size("group")
    fine_out, pooled = fine_level(
        send,
        edge_lat,
        node_lat,
        rim_a,
        rim_b,
        pool_id.reshape(1, -1),
        fine_edge_in,
        fine_edge_out,
        fine_node_in,
        fine_node_out,
        fine_bias,
        fine_gain,
        groups,
    )
    parts = lax.all_to_all(pooled, "group", 0, 0, tiled=True)
    crim = chalo_list.shape[0] // 2
    clusters = coarse_lat.shape[0]
    lists = jnp.where(odd == 1, chalo_list, jnp.roll(chalo_list, crim))
    coarse_in, coarse_proj, border = cluster_level(
        parts, coarse_lat, lists.reshape(-1, 1), coarse_edge_in
    )
    crim_a = lax.ppermute(border[:crim], "dom", inner)
    crim_b = lax.ppermute(border[crim:], "dom", outer)
    coarse_out = coarse_level(
        table_row(cedge_send, clusters, crim).reshape(-1, 1),
        cedge_lat,
        coarse_in,
        coarse_proj,
        crim_a,
        crim_b,
        coarse_edge_in,
        coarse_edge_out,
        coarse_node_in,
        coarse_node_out,
        coarse_bias,
        coarse_gain,
    )
    return (fine_out, coarse_out)


def solution(mesh):
    rows = P(("group", "dom"), None)
    flat = P(("group", "dom"))
    placed = (rows, rows, flat, flat, flat, rows, rows, flat, flat) + (P(),) * 12
    return jax.shard_map(
        body,
        mesh=mesh,
        in_specs=placed,
        out_specs=(rows, rows),
        check_vma=False,
    )
```

```python
import jax
import jax.numpy as jnp
from jax import lax
from jax.experimental import pallas as pl
from jax.experimental.pallas import tpu as pltpu
from jax.sharding import PartitionSpec as P

EPSILON = 1e-05
F32 = jnp.float32
BF16 = jnp.bfloat16
CHUNK = 1024
GATHER = 1024
TILE = 256
DEG = 4

VMEM_SPEC = pl.BlockSpec(memory_space=pltpu.VMEM)
HBM_SPEC = pl.BlockSpec(memory_space=pltpu.HBM)


def hbm(x):
    return pltpu.with_memory_space_constraint(x, pltpu.HBM)


def limit(mib):
    return pltpu.CompilerParams(vmem_limit_bytes=mib * 1024 * 1024)


def dot(a, b):
    return jnp.dot(a, b, preferred_element_type=F32)


def centred_weight(w):
    w = w.astype(F32)
    return (w - jnp.mean(w, axis=-1, keepdims=True)).astype(BF16)


def centred_row(b):
    return b - jnp.mean(b, axis=-1, keepdims=True)


def scaled_rows(z):
    mean_square = jnp.mean(z * z, axis=-1, keepdims=True)
    return z * lax.rsqrt(mean_square + EPSILON)


def store_split(table, row, values):
    n = values.shape[0]
    table[pl.ds(2 * row, n, stride=2), :] = values[:, :128]
    table[pl.ds(2 * row + 1, n, stride=2), :] = values[:, 128:]


def load_split(table, row, n):
    return jnp.concatenate(
        [table[pl.ds(2 * row, n, stride=2), :], table[pl.ds(2 * row + 1, n, stride=2), :]],
        axis=1,
    )


def border_kernel(
    list_ref, node_ref, w_ref, a_ref, b_ref, nodes, w, table, rows, index0, index1, list_sem, w_sem, node_sem
):
    rim = a_ref.shape[0]
    odd = lax.rem(lax.axis_index("dom"), 2)
    w_copy = pltpu.make_async_copy(w_ref.at[0], w, w_sem)
    w_copy.start()
    copies = [
        pltpu.make_async_copy(node_ref.at[i : i + TILE, :], nodes.at[i : i + TILE, :], node_sem.at[i // TILE])
        for i in range(0, nodes.shape[0], TILE)
    ]
    for c in copies:
        c.start()
    lists = []
    for part, (index, first) in enumerate(((index0, (1 - odd) * rim), (index1, odd * rim))):
        first = pl.multiple_of(first, rim)
        lists.append(
            pltpu.make_async_copy(list_ref.at[pl.ds(first, rim)], index, list_sem.at[part])
        )
        lists[-1].start()
    w_copy.wait()
    for i, c in enumerate(copies):
        c.wait()
        p = dot(nodes[i * TILE : (i + 1) * TILE, :], w[...])
        store_split(table, i * TILE, p.astype(BF16).astype(F32))
    for part, (index, out) in enumerate(((index1, b_ref), (index0, a_ref))):
        lists[1 - part].wait()
        for u in range(rim):
            row = pl.multiple_of(index[u] * 2, 2)
            rows[2 * u : 2 * u + 2, :] = table[pl.ds(row, 2), :]
        out[...] = load_split(rows, 0, rim).astype(BF16)


def border_rows(lists, nodes, edge_in, rim):
    shape = jax.ShapeDtypeStruct((rim, 256), BF16)
    return pl.pallas_call(
        border_kernel,
        out_shape=(shape, shape),
        in_specs=[HBM_SPEC] * 3,
        out_specs=(VMEM_SPEC, VMEM_SPEC),
        scratch_shapes=[
            pltpu.VMEM(nodes.shape, BF16),
            pltpu.VMEM((256, 256), BF16),
            pltpu.VMEM((2 * nodes.shape[0], 128), F32),
            pltpu.VMEM((2 * rim, 128), F32),
            pltpu.SMEM((rim,), jnp.int32),
            pltpu.SMEM((rim,), jnp.int32),
            pltpu.SemaphoreType.DMA((2,)),
            pltpu.SemaphoreType.DMA,
            pltpu.SemaphoreType.DMA((nodes.shape[0] // TILE,)),
        ],
        cost_estimate=pl.CostEstimate(flops=300_000_000, bytes_accessed=2_000_000, transcendentals=0),
        name="border_rows",
        compiler_params=limit(10),
    )(hbm(lists), hbm(nodes), hbm(edge_in))


def edges_kernel(
    send_hbm,
    pool_hbm,
    node_hbm,
    edge_in_hbm,
    edge_out_hbm,
    node_in_hbm,
    node_out_hbm,
    bias_hbm,
    edge_hbm,
    pre_ref,
    own_ref,
    table_ref,
    row_ref,
    w_ref,
    member_ref,
    count_ref,
    send,
    pool,
    node,
    edge_in,
    edge_out,
    node_in,
    node_out,
    bias,
    edges,
    rep0,
    rep1,
    small_sem,
    edge_sem,
):
    nodes = node.shape[0]
    chunks = edges.shape[0] // CHUNK
    cnodes = CHUNK // DEG
    rim = (table_ref.shape[0] // 2 - nodes) // 2
    small = [
        pltpu.make_async_copy(source, target, small_sem.at[i])
        for i, (source, target) in enumerate(
            (
                (send_hbm, send),
                (pool_hbm, pool),
                (node_hbm, node),
                (edge_in_hbm, edge_in),
                (edge_out_hbm, edge_out),
                (node_in_hbm, node_in),
                (node_out_hbm, node_out),
                (bias_hbm, bias),
            )
        )
    ]
    copies = [
        pltpu.make_async_copy(
            edge_hbm.at[c * CHUNK : (c + 1) * CHUNK, :],
            edges.at[c * CHUNK : (c + 1) * CHUNK, :],
            edge_sem.at[c],
        )
        for c in range(chunks)
    ]
    for c in small + copies:
        c.start()
    for c in small:
        c.wait()
    odd = lax.rem(lax.axis_index("dom"), 2)
    sent = send[...]
    lower = jnp.where(odd == 1, nodes, nodes + rim)
    upper = jnp.where(odd == 1, nodes + rim, nodes) - (rim + nodes)
    row_ref[...] = 2 * (
        sent + jnp.where(sent < rim, lower, jnp.where(sent < rim + nodes, -rim, upper))
    )
    w_ref[0] = centred_weight(edge_out[...])
    w_ref[1] = centred_weight(node_out[...])
    b_edge = bias[0:1, :]
    b_node = bias[2:3, :]

    def own_terms(k, carry):
        i = pl.multiple_of(k * CHUNK, CHUNK)
        own = node[pl.ds(i, CHUNK), :]
        store_split(table_ref, i, dot(own, edge_in[0]).astype(BF16).astype(F32))
        own_ref[pl.ds(i, CHUNK), :] = dot(own, node_in[0]) + b_node
        return carry

    lax.fori_loop(0, nodes // CHUNK, own_terms, 0, unroll=True)

    def edge_chunk(c, carry):
        own = node[pl.ds(pl.multiple_of(c * cnodes, cnodes), cnodes), :]
        receiver = dot(own, edge_in[1]) + b_edge
        for j in range(DEG):
            rep0[pl.ds(j, cnodes, stride=DEG), :] = receiver[:, :128]
            rep1[pl.ds(j, cnodes, stride=DEG), :] = receiver[:, 128:]
        at = pl.ds(pl.multiple_of(c * CHUNK, CHUNK), CHUNK)
        pltpu.make_async_copy(edge_hbm.at[at, :], edges.at[at, :], edge_sem.at[c]).wait()
        pre_ref[at, :] = dot(edges[at, :], edge_in[2]) + jnp.concatenate(
            [rep0[...], rep1[...]], axis=1
        )
        return carry

    lax.fori_loop(0, chunks, edge_chunk, 0, unroll=2)

    ids = pool[...]
    lane = lax.broadcasted_iota(jnp.int32, (256, 128), 1)

    def membership(g, carry):
        member = (
            lax.broadcasted_iota(jnp.int32, (256, nodes), 0) + g * 256 == ids
        ).astype(F32)
        member_ref[g] = member.astype(BF16)
        count = jnp.sum(member, axis=1, keepdims=True)
        high = jnp.floor(count * (1.0 / 256.0))
        low = count - high * 256.0
        both = jnp.where(lane == 0, low, jnp.where(lane == 1, high, 0.0))
        count_ref[g] = both.T[:16, :].astype(BF16)
        return carry

    lax.fori_loop(0, member_ref.shape[0], membership, 0)


def edge_terms(send, pool, edges, nodes, rim, owners, edge_in, edge_out, node_in, node_out, bias):
    n = nodes.shape[0]
    e = edges.shape[0]
    shape = jax.ShapeDtypeStruct
    operands = (send, pool, nodes, edge_in, edge_out, node_in, node_out, bias, edges)
    return pl.pallas_call(
        edges_kernel,
        out_shape=(
            shape((e, 256), F32),
            shape((n, 256), F32),
            shape((2 * (n + 2 * rim), 128), F32),
            shape(send.shape, jnp.int32),
            shape((2, 256, 256), BF16),
            shape((owners, 256, n), BF16),
            shape((owners, 16, 256), BF16),
        ),
        in_specs=[HBM_SPEC] * len(operands),
        out_specs=(VMEM_SPEC,) * 7,
        scratch_shapes=[pltpu.VMEM(x.shape, x.dtype) for x in operands]
        + [
            pltpu.VMEM((CHUNK, 128), F32),
            pltpu.VMEM((CHUNK, 128), F32),
            pltpu.SemaphoreType.DMA((8,)),
            pltpu.SemaphoreType.DMA((e // CHUNK,)),
        ],
        cost_estimate=pl.CostEstimate(flops=3_000_000_000, bytes_accessed=8_000_000, transcendentals=0),
        name="edge_terms",
        compiler_params=limit(14),
    )(*(hbm(x) for x in operands))


def fine_kernel(
    row_ref,
    pre_ref,
    own_ref,
    table_ref,
    w_ref,
    member_ref,
    count_ref,
    low_ref,
    high_ref,
    node_hbm,
    node_in,
    bias,
    gain,
    out_hbm,
    pooled_ref,
    table,
    rows,
    node,
    out,
    summed,
    index,
    index_sem,
    node_sem,
    out_sem,
):
    nodes = node.shape[0]
    chunks = pre_ref.shape[0] // GATHER
    rim = low_ref.shape[0]
    cnodes = GATHER // DEG
    lines = GATHER // 128

    def index_copy(c):
        at = pl.ds(pl.multiple_of(c * lines, lines), lines)
        return pltpu.make_async_copy(row_ref.at[at, :], index, index_sem)

    index_copy(0).start()
    node_copy = pltpu.make_async_copy(node_hbm, node, node_sem)
    node_copy.start()
    store_split(table, nodes, low_ref[...].astype(F32))
    store_split(table, nodes + rim, high_ref[...].astype(F32))
    b_message = centred_row(bias[1:2, :])
    b_update = centred_row(bias[3:4, :])
    g_message = gain[0:1, :]
    g_update = gain[1:2, :]
    tnodes = TILE // DEG
    collect = (
        lax.broadcasted_iota(jnp.int32, (tnodes, TILE), 1) // DEG
        == lax.broadcasted_iota(jnp.int32, (tnodes, TILE), 0)
    ).astype(F32).astype(BF16)

    def chunk(c, carry):
        index_copy(c).wait()
        for u in range(GATHER):
            row = pl.multiple_of(index[u // 128, u % 128], 2)
            rows[2 * u : 2 * u + 2, :] = table[pl.ds(row, 2), :]
        index_copy(jnp.minimum(c + 1, chunks - 1)).start()
        pre = pre_ref[pl.ds(pl.multiple_of(c * GATHER, GATHER), GATHER), :]
        hidden = jnp.maximum(pre + load_split(rows, 0, GATHER), 0.0).astype(BF16)
        m = scaled_rows(dot(hidden, w_ref[0]) + b_message).astype(BF16)
        sums = [dot(collect, m[q : q + TILE, :]) for q in range(0, GATHER, TILE)]
        summed[pl.ds(pl.multiple_of(c * cnodes, cnodes), cnodes), :] = (
            jnp.concatenate(sums, axis=0) * g_message
        ).astype(BF16)
        return carry

    lax.fori_loop(0, chunks, chunk, 0)
    index_copy(0).wait()
    node_copy.wait()
    hidden = jnp.maximum(own_ref[...] + dot(summed[...], node_in[1]), 0.0).astype(BF16)
    u = scaled_rows(dot(hidden, w_ref[1]) + b_update) * g_update
    out[...] = (node[...].astype(F32) + u).astype(BF16)
    out_copy = pltpu.make_async_copy(out, out_hbm, out_sem)
    out_copy.start()
    for g in range(pooled_ref.shape[0]):
        pooled_ref[g, :256, :] = dot(member_ref[g], out[...]).astype(BF16)
        pooled_ref[g, 256:, :] = count_ref[g]
    out_copy.wait()


def fine_level(terms, nodes, low, high, node_in, bias, gain):
    n = nodes.shape[0]
    pre, own, table, row, w, member, count = terms
    owners = member.shape[0]
    outs = pl.pallas_call(
        fine_kernel,
        out_shape=(
            jax.ShapeDtypeStruct((n, 256), BF16),
            jax.ShapeDtypeStruct((owners, 272, 256), BF16),
            jax.ShapeDtypeStruct(table.shape, F32),
        ),
        in_specs=[VMEM_SPEC] * 9 + [HBM_SPEC] + [VMEM_SPEC] * 3,
        out_specs=(HBM_SPEC, VMEM_SPEC, VMEM_SPEC),
        scratch_shapes=[
            pltpu.VMEM((2 * GATHER, 128), F32),
            pltpu.VMEM((n, 256), BF16),
            pltpu.VMEM((n, 256), BF16),
            pltpu.VMEM((n, 256), BF16),
            pltpu.SMEM((GATHER // 128, 128), jnp.int32),
            pltpu.SemaphoreType.DMA,
            pltpu.SemaphoreType.DMA,
            pltpu.SemaphoreType.DMA,
        ],
        input_output_aliases={3: 2},
        cost_estimate=pl.CostEstimate(flops=4_000_000_000, bytes_accessed=8_000_000, transcendentals=0),
        name="fine_level",
        compiler_params=limit(16),
    )(row, pre, own, table, w, member, count, low, high, hbm(nodes), node_in, bias, gain)
    return outs[0], outs[1]


def one_hot_rows(index_col, count):
    return (
        index_col == lax.broadcasted_iota(jnp.int32, (index_col.shape[0], count), 1)
    ).astype(F32).astype(BF16)


def cluster_kernel(parts_ref, lat_ref, list_ref, w_ref, in_ref, proj_ref, a_ref, b_ref):
    clusters = lat_ref.shape[0]
    rim = a_ref.shape[0]
    total = parts_ref[0, :clusters, :].astype(F32)
    tail = parts_ref[0, clusters:, :].astype(F32)
    for g in range(1, parts_ref.shape[0]):
        total = total + parts_ref[g, :clusters, :].astype(F32)
        tail = tail + parts_ref[g, clusters:, :].astype(F32)
    count = tail[0:1, :] + 256.0 * tail[1:2, :]
    count = jnp.broadcast_to(count, (8, clusters)).T[:, :1]
    mean = total / jnp.maximum(count, 1.0)
    coarse_in = (lat_ref[...].astype(F32) + mean).astype(BF16)
    in_ref[...] = coarse_in
    proj = dot(coarse_in, w_ref[0]).astype(BF16)
    proj_ref[...] = proj
    border = dot(one_hot_rows(list_ref[...], clusters), proj).astype(BF16)
    a_ref[...] = border[:rim, :]
    b_ref[...] = border[rim:, :]


def cluster_level(parts, lat, lists, edge_in):
    n = lat.shape[0]
    shape = jax.ShapeDtypeStruct((n, 256), BF16)
    rim = jax.ShapeDtypeStruct((lists.shape[0] // 2, 256), BF16)
    return pl.pallas_call(
        cluster_kernel,
        out_shape=(shape, shape, rim, rim),
        in_specs=[VMEM_SPEC] * 4,
        out_specs=(VMEM_SPEC,) * 4,
        cost_estimate=pl.CostEstimate(flops=70_000_000, bytes_accessed=1_000_000, transcendentals=0),
        name="cluster_level",
        compiler_params=limit(16),
    )(parts, lat, lists, edge_in)


def coarse_edges_kernel(send_ref, edge_ref, node_ref, proj_ref, edge_in, edge_out, node_in, node_out, bias, pre_ref, own_ref, w_ref):
    nodes = node_ref.shape[0]
    count = edge_ref.shape[0]
    own = node_ref[...]
    receiver = (dot(own, edge_in[1]) + bias[0:1, :]).astype(BF16)
    spread = (
        lax.broadcasted_iota(jnp.int32, (count, nodes), 0) // DEG
        == lax.broadcasted_iota(jnp.int32, (count, nodes), 1)
    ).astype(F32).astype(BF16)
    picked = one_hot_rows(send_ref[...], nodes)
    pre_ref[...] = dot(edge_ref[...], edge_in[2]) + (dot(spread, receiver) + dot(picked, proj_ref[...]))
    own_ref[...] = dot(own, node_in[0]) + bias[2:3, :]
    w_ref[0] = centred_weight(edge_out[...])
    w_ref[1] = centred_weight(node_out[...])


def coarse_edge_terms(send, edges, nodes, proj, edge_in, edge_out, node_in, node_out, bias):
    shape = jax.ShapeDtypeStruct
    return pl.pallas_call(
        coarse_edges_kernel,
        out_shape=(shape(edges.shape, F32), shape(nodes.shape, F32), shape((2, 256, 256), BF16)),
        in_specs=[VMEM_SPEC] * 9,
        out_specs=(VMEM_SPEC,) * 3,
        cost_estimate=pl.CostEstimate(flops=500_000_000, bytes_accessed=3_000_000, transcendentals=0),
        name="coarse_edge_terms",
        compiler_params=limit(16),
    )(send, edges, nodes, proj, edge_in, edge_out, node_in, node_out, bias)


def coarse_kernel(send_ref, pre_ref, own_ref, w_ref, node_ref, low_ref, high_ref, node_in, bias, gain, out_ref):
    nodes = node_ref.shape[0]
    rim = low_ref.shape[0]
    count = pre_ref.shape[0]
    rims = jnp.concatenate([low_ref[...], high_ref[...]], axis=0)
    b_message = centred_row(bias[1:2, :])
    b_update = centred_row(bias[3:4, :])
    tnodes = TILE // DEG
    collect = (
        lax.broadcasted_iota(jnp.int32, (tnodes, TILE), 1) // DEG
        == lax.broadcasted_iota(jnp.int32, (tnodes, TILE), 0)
    ).astype(F32).astype(BF16)
    picked = one_hot_rows(send_ref[...] - nodes, 2 * rim)
    hidden = jnp.maximum(pre_ref[...] + dot(picked, rims), 0.0).astype(BF16)
    m = scaled_rows(dot(hidden, w_ref[0]) + b_message).astype(BF16)
    sums = [dot(collect, m[q : q + TILE, :]) for q in range(0, count, TILE)]
    summed = (jnp.concatenate(sums, axis=0) * gain[0:1, :]).astype(BF16)
    hidden = jnp.maximum(own_ref[...] + dot(summed, node_in[1]), 0.0).astype(BF16)
    u = scaled_rows(dot(hidden, w_ref[1]) + b_update) * gain[1:2, :]
    out_ref[...] = (node_ref[...].astype(F32) + u).astype(BF16)


def coarse_level(send, terms, nodes, low, high, node_in, bias, gain):
    pre, own, w = terms
    return pl.pallas_call(
        coarse_kernel,
        out_shape=jax.ShapeDtypeStruct(nodes.shape, BF16),
        in_specs=[VMEM_SPEC] * 10,
        out_specs=VMEM_SPEC,
        cost_estimate=pl.CostEstimate(flops=500_000_000, bytes_accessed=3_000_000, transcendentals=0),
        name="coarse_level",
        compiler_params=limit(16),
    )(send, pre, own, w, nodes, low, high, node_in, bias, gain)


def pair_swaps():
    count = lax.axis_size("dom")
    inner = [(i, i ^ 1) for i in range(count)]
    outer = [(i, ((i + 1) ^ 1) - 1) for i in range(1, count - 1)]
    return inner, outer


def body(
    node_lat,
    edge_lat,
    edge_send,
    halo_list,
    pool_id,
    coarse_lat,
    cedge_lat,
    cedge_send,
    chalo_list,
    fine_edge_in,
    fine_edge_out,
    fine_node_in,
    fine_node_out,
    fine_bias,
    fine_gain,
    coarse_edge_in,
    coarse_edge_out,
    coarse_node_in,
    coarse_node_out,
    coarse_bias,
    coarse_gain,
):
    inner, outer = pair_swaps()
    odd = lax.rem(lax.axis_index("dom"), 2)
    rim = halo_list.shape[0] // 2

    def table_row(send, count, rim_rows):
        lower = jnp.where(odd == 1, count, count + rim_rows)
        upper = jnp.where(odd == 1, count + rim_rows, count)
        return jnp.where(
            send < rim_rows,
            send + lower,
            jnp.where(
                send < rim_rows + count, send - rim_rows, send - (rim_rows + count) + upper
            ),
        )

    border_a, border_b = border_rows(halo_list, node_lat, fine_edge_in, rim)
    rim_a = lax.ppermute(border_a, "dom", inner)
    rim_b = lax.ppermute(border_b, "dom", outer)
    groups = lax.axis_size("group")
    terms = edge_terms(
        edge_send.reshape(-1, 128),
        pool_id.reshape(1, -1),
        edge_lat,
        node_lat,
        rim,
        groups,
        fine_edge_in,
        fine_edge_out,
        fine_node_in,
        fine_node_out,
        fine_bias,
    )
    fine_out, pooled = fine_level(
        terms, node_lat, rim_a, rim_b, fine_node_in, fine_bias, fine_gain
    )
    parts = lax.all_to_all(pooled, "group", 0, 0, tiled=True)
    crim = chalo_list.shape[0] // 2
    clusters = coarse_lat.shape[0]
    lists = jnp.where(odd == 1, chalo_list, jnp.roll(chalo_list, crim))
    coarse_in, coarse_proj, cborder_a, cborder_b = cluster_level(
        parts, coarse_lat, lists.reshape(-1, 1), coarse_edge_in
    )
    crim_a = lax.ppermute(cborder_a, "dom", inner)
    crim_b = lax.ppermute(cborder_b, "dom", outer)
    csend = table_row(cedge_send, clusters, crim).reshape(-1, 1)
    cterms = coarse_edge_terms(
        csend,
        cedge_lat,
        coarse_in,
        coarse_proj,
        coarse_edge_in,
        coarse_edge_out,
        coarse_node_in,
        coarse_node_out,
        coarse_bias,
    )
    coarse_out = coarse_level(
        csend, cterms, coarse_in, crim_a, crim_b, coarse_node_in, coarse_bias, coarse_gain
    )
    return (fine_out, coarse_out)


def solution(mesh):
    rows = P(("group", "dom"), None)
    flat = P(("group", "dom"))
    placed = (rows, rows, flat, flat, flat, rows, rows, flat, flat) + (P(),) * 12
    return jax.shard_map(
        body,
        mesh=mesh,
        in_specs=placed,
        out_specs=(rows, rows),
        check_vma=False,
    )
```

```python
import jax
import jax.numpy as jnp
from jax import lax
from jax.experimental import pallas as pl
from jax.experimental.pallas import tpu as pltpu
from jax.sharding import PartitionSpec as P

EPSILON = 1e-05
F32 = jnp.float32
BF16 = jnp.bfloat16
CHUNK = 1024
GATHER = 1024
TILE = 256
DEG = 4

VMEM_SPEC = pl.BlockSpec(memory_space=pltpu.VMEM)
HBM_SPEC = pl.BlockSpec(memory_space=pltpu.HBM)


def hbm(x):
    return pltpu.with_memory_space_constraint(x, pltpu.HBM)


def limit(mib):
    return pltpu.CompilerParams(vmem_limit_bytes=mib * 1024 * 1024)


def dot(a, b):
    return jnp.dot(a, b, preferred_element_type=F32)


def centred_weight(w):
    w = w.astype(F32)
    return (w - jnp.mean(w, axis=-1, keepdims=True)).astype(BF16)


def centred_row(b):
    return b - jnp.mean(b, axis=-1, keepdims=True)


def scaled_rows(z):
    mean_square = jnp.mean(z * z, axis=-1, keepdims=True)
    return z * lax.rsqrt(mean_square + EPSILON)


def store_split(table, row, values):
    n = values.shape[0]
    table[pl.ds(2 * row, n, stride=2), :] = values[:, :128]
    table[pl.ds(2 * row + 1, n, stride=2), :] = values[:, 128:]


def load_split(table, row, n):
    return jnp.concatenate(
        [table[pl.ds(2 * row, n, stride=2), :], table[pl.ds(2 * row + 1, n, stride=2), :]],
        axis=1,
    )


def copy_rows(table, rows, index, count):
    for u in range(count):
        row = pl.multiple_of(index[u] * 2, 2)
        rows[2 * u : 2 * u + 2, :] = table[pl.ds(row, 2), :]


def border_kernel(
    list_ref, node_ref, w_ref, b_ref, nodes, w, table, rows, index, list_sem, w_sem, node_sem
):
    rim = b_ref.shape[0]
    odd = lax.rem(lax.axis_index("dom"), 2)
    copies = [
        pltpu.make_async_copy(node_ref.at[i : i + TILE, :], nodes.at[i : i + TILE, :], node_sem.at[i // TILE])
        for i in range(0, nodes.shape[0], TILE)
    ]
    for c in copies:
        c.start()
    first = pl.multiple_of(odd * rim, rim)
    list_copy = pltpu.make_async_copy(list_ref.at[pl.ds(first, rim)], index, list_sem)
    list_copy.start()
    w_copy = pltpu.make_async_copy(w_ref, w, w_sem)
    w_copy.start()
    for i, c in enumerate(copies):
        c.wait()
        store_split(table, i * TILE, nodes[i * TILE : (i + 1) * TILE, :].astype(F32))
    list_copy.wait()
    copy_rows(table, rows, index, rim)
    w_copy.wait()
    b_ref[...] = dot(load_split(rows, 0, rim).astype(BF16), w[0]).astype(BF16)


def border_rows(lists, nodes, edge_in, rim):
    shape = jax.ShapeDtypeStruct
    return pl.pallas_call(
        border_kernel,
        out_shape=(
            shape((rim, 256), BF16),
            shape(nodes.shape, BF16),
            shape(edge_in.shape, BF16),
        ),
        in_specs=[HBM_SPEC] * 3,
        out_specs=(VMEM_SPEC,) * 3,
        scratch_shapes=[
            pltpu.VMEM((2 * nodes.shape[0], 128), F32),
            pltpu.VMEM((2 * rim, 128), F32),
            pltpu.SMEM((rim,), jnp.int32),
            pltpu.SemaphoreType.DMA,
            pltpu.SemaphoreType.DMA,
            pltpu.SemaphoreType.DMA((nodes.shape[0] // TILE,)),
        ],
        cost_estimate=pl.CostEstimate(flops=70_000_000, bytes_accessed=2_000_000, transcendentals=0),
        name="border_rows",
        compiler_params=limit(8),
    )(hbm(lists), hbm(nodes), hbm(edge_in))


def own_kernel(list_ref, node_ref, w_ref, a_ref, table, rows, index, list_sem):
    rim = a_ref.shape[0]
    odd = lax.rem(lax.axis_index("dom"), 2)
    first = pl.multiple_of((1 - odd) * rim, rim)
    list_copy = pltpu.make_async_copy(list_ref.at[pl.ds(first, rim)], index, list_sem)
    list_copy.start()
    store_split(table, 0, node_ref[...].astype(F32))
    list_copy.wait()
    copy_rows(table, rows, index, rim)
    a_ref[...] = dot(load_split(rows, 0, rim).astype(BF16), w_ref[0]).astype(BF16)


def own_rows(lists, nodes, edge_in, rim):
    return pl.pallas_call(
        own_kernel,
        out_shape=jax.ShapeDtypeStruct((rim, 256), BF16),
        in_specs=[HBM_SPEC] + [VMEM_SPEC] * 2,
        out_specs=VMEM_SPEC,
        scratch_shapes=[
            pltpu.VMEM((2 * nodes.shape[0], 128), F32),
            pltpu.VMEM((2 * rim, 128), F32),
            pltpu.SMEM((rim,), jnp.int32),
            pltpu.SemaphoreType.DMA,
        ],
        cost_estimate=pl.CostEstimate(flops=70_000_000, bytes_accessed=2_000_000, transcendentals=0),
        name="own_rows",
        compiler_params=limit(8),
    )(hbm(lists), nodes, edge_in)


def edges_kernel(
    node,
    edge_in,
    send_hbm,
    pool_hbm,
    edge_out_hbm,
    node_in_hbm,
    node_out_hbm,
    bias_hbm,
    edge_hbm,
    pre_ref,
    own_ref,
    row_ref,
    w_ref,
    member_ref,
    count_ref,
    table_ref,
    send,
    pool,
    edge_out,
    node_in,
    node_out,
    bias,
    edges,
    rep0,
    rep1,
    small_sem,
    edge_sem,
):
    nodes = node.shape[0]
    chunks = edges.shape[0] // CHUNK
    cnodes = CHUNK // DEG
    rim = (table_ref.shape[0] // 2 - nodes) // 2
    small = [
        pltpu.make_async_copy(source, target, small_sem.at[i])
        for i, (source, target) in enumerate(
            (
                (bias_hbm, bias),
                (pool_hbm, pool),
                (send_hbm, send),
                (edge_out_hbm, edge_out),
                (node_in_hbm, node_in),
                (node_out_hbm, node_out),
            )
        )
    ]
    copies = [
        pltpu.make_async_copy(
            edge_hbm.at[c * CHUNK : (c + 1) * CHUNK, :],
            edges.at[c * CHUNK : (c + 1) * CHUNK, :],
            edge_sem.at[c],
        )
        for c in range(chunks)
    ]
    for c in small + copies:
        c.start()
    small[0].wait()
    small[1].wait()

    me = lax.axis_index("group")
    owners = member_ref.shape[0]
    ids = pool[...]
    row = lax.broadcasted_iota(jnp.int32, (256, 128), 0).astype(F32).astype(BF16)
    lane = lax.broadcasted_iota(jnp.int32, (256, 128), 1)
    one = jnp.ones((256, 128), BF16)
    zero = jnp.zeros((256, 128), BF16)
    for k, step in enumerate((2, 1, 3, 0)):
        base = lax.rem(me + step, owners) * 256
        local = ids - base
        inside = jnp.logical_and(local >= 0, local < 256)
        local = jnp.where(inside, local, 256).astype(F32).astype(BF16)
        total = zero
        for i in range(0, nodes, 128):
            here = jnp.broadcast_to(local[:, i : i + 128], (256, 128))
            member = jnp.where(row == here, one, zero)
            member_ref[k, :, i : i + 128] = member
            total = total + member
        count = jnp.sum(total.astype(F32), axis=1, keepdims=True)
        high = jnp.floor(count * (1.0 / 64.0))
        low = count - high * 64.0
        both = jnp.where(lane == 0, low, jnp.where(lane == 1, high, 0.0))
        count_ref[k] = both.T[:16, :].astype(BF16)

    b_edge = bias[0:1, :]
    b_node = bias[2:3, :]

    def edge_chunk(c, carry):
        own = node[pl.ds(pl.multiple_of(c * cnodes, cnodes), cnodes), :]
        receiver = dot(own, edge_in[1]) + b_edge
        for j in range(DEG):
            rep0[pl.ds(j, cnodes, stride=DEG), :] = receiver[:, :128]
            rep1[pl.ds(j, cnodes, stride=DEG), :] = receiver[:, 128:]
        at = pl.ds(pl.multiple_of(c * CHUNK, CHUNK), CHUNK)
        pltpu.make_async_copy(edge_hbm.at[at, :], edges.at[at, :], edge_sem.at[c]).wait()
        pre_ref[at, :] = dot(edges[at, :], edge_in[2]) + jnp.concatenate(
            [rep0[...], rep1[...]], axis=1
        )
        return carry

    lax.fori_loop(0, chunks, edge_chunk, 0, unroll=2)

    for c in small[2:]:
        c.wait()
    odd = lax.rem(lax.axis_index("dom"), 2)
    sent = send[...]
    lower = jnp.where(odd == 1, nodes, nodes + rim)
    upper = jnp.where(odd == 1, nodes + rim, nodes) - (rim + nodes)
    row_ref[...] = 2 * (
        sent + jnp.where(sent < rim, lower, jnp.where(sent < rim + nodes, -rim, upper))
    )
    w_ref[0] = centred_weight(edge_out[...])
    w_ref[1] = centred_weight(node_out[...])
    for i in range(0, nodes, CHUNK):
        own = node[i : i + CHUNK, :]
        store_split(table_ref, i, dot(own, edge_in[0]).astype(BF16).astype(F32))
        own_ref[i : i + CHUNK, :] = dot(own, node_in[0]) + b_node


def edge_terms(send, pool, edges, nodes, rim, owners, edge_in, edge_out, node_in, node_out, bias):
    n = nodes.shape[0]
    e = edges.shape[0]
    shape = jax.ShapeDtypeStruct
    operands = (send, pool, edge_out, node_in, node_out, bias, edges)
    return pl.pallas_call(
        edges_kernel,
        out_shape=(
            shape((e, 256), F32),
            shape((n, 256), F32),
            shape(send.shape, jnp.int32),
            shape((2, 256, 256), BF16),
            shape((owners, 256, n), BF16),
            shape((owners, 16, 256), BF16),
            shape((2 * (n + 2 * rim), 128), F32),
        ),
        in_specs=[VMEM_SPEC] * 2 + [HBM_SPEC] * len(operands),
        out_specs=(VMEM_SPEC,) * 7,
        scratch_shapes=[pltpu.VMEM(x.shape, x.dtype) for x in operands]
        + [
            pltpu.VMEM((CHUNK, 128), F32),
            pltpu.VMEM((CHUNK, 128), F32),
            pltpu.SemaphoreType.DMA((6,)),
            pltpu.SemaphoreType.DMA((e // CHUNK,)),
        ],
        cost_estimate=pl.CostEstimate(flops=3_000_000_000, bytes_accessed=8_000_000, transcendentals=0),
        name="edge_terms",
        compiler_params=limit(14),
    )(nodes, edge_in, *(hbm(x) for x in operands))


def fine_kernel(
    row_ref,
    pre_ref,
    own_ref,
    table_ref,
    w_ref,
    member_ref,
    count_ref,
    low_ref,
    high_ref,
    node,
    node_in,
    bias,
    gain,
    out_hbm,
    out,
    up_ref,
    down_ref,
    table,
    rows,
    summed,
    index0,
    index1,
    index_sem,
    out_sem,
):
    nodes = node.shape[0]
    chunks = pre_ref.shape[0] // GATHER
    rim = low_ref.shape[0]
    cnodes = GATHER // DEG
    lines = GATHER // 128

    def index_copy(c, slot):
        c = jnp.minimum(c, chunks - 1)
        at = pl.ds(pl.multiple_of(c * lines, lines), lines)
        return pltpu.make_async_copy(
            row_ref.at[at, :], index1 if slot else index0, index_sem.at[slot]
        )

    index_copy(0, 0).start()
    index_copy(1, 1).start()
    store_split(table, nodes, low_ref[...].astype(F32))
    store_split(table, nodes + rim, high_ref[...].astype(F32))
    b_message = centred_row(bias[1:2, :])
    b_update = centred_row(bias[3:4, :])
    g_message = gain[0:1, :]
    g_update = gain[1:2, :]
    tnodes = TILE // DEG
    collect = (
        lax.broadcasted_iota(jnp.int32, (tnodes, TILE), 1) // DEG
        == lax.broadcasted_iota(jnp.int32, (tnodes, TILE), 0)
    ).astype(F32).astype(BF16)

    def pair(k, carry):
        for slot, index in enumerate((index0, index1)):
            c = 2 * k + slot
            index_copy(c, slot).wait()
            for u in range(GATHER):
                row = pl.multiple_of(index[u // 128, u % 128], 2)
                rows[2 * u : 2 * u + 2, :] = table[pl.ds(row, 2), :]
            index_copy(c + 2, slot).start()
            pre = pre_ref[pl.ds(pl.multiple_of(c * GATHER, GATHER), GATHER), :]
            hidden = jnp.maximum(pre + load_split(rows, 0, GATHER), 0.0).astype(BF16)
            m = scaled_rows(dot(hidden, w_ref[0]) + b_message).astype(BF16)
            sums = [dot(collect, m[q : q + TILE, :]) for q in range(0, GATHER, TILE)]
            summed[pl.ds(pl.multiple_of(c * cnodes, cnodes), cnodes), :] = (
                jnp.concatenate(sums, axis=0) * g_message
            ).astype(BF16)
        return carry

    lax.fori_loop(0, chunks // 2, pair, 0)
    index_copy(0, 0).wait()
    index_copy(1, 1).wait()
    hidden = jnp.maximum(own_ref[...] + dot(summed[...], node_in[1]), 0.0).astype(BF16)
    u = scaled_rows(dot(hidden, w_ref[1]) + b_update) * g_update
    out[...] = (node[...].astype(F32) + u).astype(BF16)
    out_copy = pltpu.make_async_copy(out, out_hbm, out_sem)
    out_copy.start()
    far = dot(member_ref[0], out[...]).astype(BF16)
    up_ref[:256, :] = far[:, :128]
    down_ref[:256, :] = far[:, 128:]
    up_ref[256:, :] = count_ref[0, :, :128]
    down_ref[256:, :] = count_ref[0, :, 128:]
    out_copy.wait()


def fine_level(terms, table, nodes, low, high, node_in, bias, gain):
    n = nodes.shape[0]
    pre, own, row, w, member, count = terms
    shape = jax.ShapeDtypeStruct
    outs = pl.pallas_call(
        fine_kernel,
        out_shape=(
            shape((n, 256), BF16),
            shape((n, 256), BF16),
            shape((272, 128), BF16),
            shape((272, 128), BF16),
            shape(table.shape, F32),
        ),
        in_specs=[VMEM_SPEC] * 13,
        out_specs=(HBM_SPEC,) + (VMEM_SPEC,) * 4,
        scratch_shapes=[
            pltpu.VMEM((2 * GATHER, 128), F32),
            pltpu.VMEM((n, 256), BF16),
            pltpu.SMEM((GATHER // 128, 128), jnp.int32),
            pltpu.SMEM((GATHER // 128, 128), jnp.int32),
            pltpu.SemaphoreType.DMA((2,)),
            pltpu.SemaphoreType.DMA,
        ],
        input_output_aliases={3: 4},
        cost_estimate=pl.CostEstimate(flops=4_000_000_000, bytes_accessed=8_000_000, transcendentals=0),
        name="fine_level",
        compiler_params=limit(14),
    )(row, pre, own, table, w, member, count, low, high, nodes, node_in, bias, gain)
    return outs[:4]


def pool_kernel(member_ref, count_ref, out_ref, next_ref, prev_ref, mine_ref):
    for k, ref in enumerate((next_ref, prev_ref, mine_ref)):
        ref[:256, :] = dot(member_ref[k + 1], out_ref[...]).astype(BF16)
        ref[256:, :] = count_ref[k + 1]


def pool_rows(member, count, out):
    shape = jax.ShapeDtypeStruct((272, 256), BF16)
    return pl.pallas_call(
        pool_kernel,
        out_shape=(shape,) * 3,
        in_specs=[VMEM_SPEC] * 3,
        out_specs=(VMEM_SPEC,) * 3,
        cost_estimate=pl.CostEstimate(flops=800_000_000, bytes_accessed=4_000_000, transcendentals=0),
        name="pool_rows",
        compiler_params=limit(8),
    )(member, count, out)


def relay_kernel(next_ref, prev_ref, up_ref, down_ref, next_out, prev_out):
    next_out[:, :128] = (next_ref[:, :128].astype(F32) + up_ref[...].astype(F32)).astype(BF16)
    next_out[:, 128:] = next_ref[:, 128:]
    prev_out[:, :128] = prev_ref[:, :128]
    prev_out[:, 128:] = (prev_ref[:, 128:].astype(F32) + down_ref[...].astype(F32)).astype(BF16)


def relay_rows(next_rows, prev_rows, up, down):
    shape = jax.ShapeDtypeStruct((272, 256), BF16)
    return pl.pallas_call(
        relay_kernel,
        out_shape=(shape,) * 2,
        in_specs=[VMEM_SPEC] * 4,
        out_specs=(VMEM_SPEC,) * 2,
        cost_estimate=pl.CostEstimate(flops=200_000, bytes_accessed=1_000_000, transcendentals=0),
        name="relay_rows",
        compiler_params=limit(8),
    )(next_rows, prev_rows, up, down)


def one_hot_rows(index_col, count):
    return (
        index_col == lax.broadcasted_iota(jnp.int32, (index_col.shape[0], count), 1)
    ).astype(F32).astype(BF16)


def cluster_kernel(mine_ref, below_ref, above_ref, lat_ref, list_ref, w_ref, in_ref, proj_ref, a_ref, b_ref):
    clusters = lat_ref.shape[0]
    rim = a_ref.shape[0]
    total = mine_ref[...].astype(F32) + below_ref[...].astype(F32) + above_ref[...].astype(F32)
    count = total[clusters : clusters + 1, :] + 64.0 * total[clusters + 1 : clusters + 2, :]
    total = total[:clusters, :]
    count = jnp.broadcast_to(count, (8, clusters)).T[:, :1]
    mean = total / jnp.maximum(count, 1.0)
    coarse_in = (lat_ref[...].astype(F32) + mean).astype(BF16)
    in_ref[...] = coarse_in
    proj = dot(coarse_in, w_ref[0]).astype(BF16)
    proj_ref[...] = proj
    border = dot(one_hot_rows(list_ref[...], clusters), proj).astype(BF16)
    a_ref[...] = border[:rim, :]
    b_ref[...] = border[rim:, :]


def cluster_level(mine, below, above, lat, lists, edge_in):
    n = lat.shape[0]
    shape = jax.ShapeDtypeStruct((n, 256), BF16)
    rim = jax.ShapeDtypeStruct((lists.shape[0] // 2, 256), BF16)
    return pl.pallas_call(
        cluster_kernel,
        out_shape=(shape, shape, rim, rim),
        in_specs=[VMEM_SPEC] * 6,
        out_specs=(VMEM_SPEC,) * 4,
        cost_estimate=pl.CostEstimate(flops=70_000_000, bytes_accessed=1_000_000, transcendentals=0),
        name="cluster_level",
        compiler_params=limit(16),
    )(mine, below, above, lat, lists, edge_in)


def coarse_edges_kernel(send_ref, edge_ref, node_ref, proj_ref, edge_in, edge_out, node_in, node_out, bias, pre_ref, own_ref, w_ref):
    nodes = node_ref.shape[0]
    count = edge_ref.shape[0]
    own = node_ref[...]
    receiver = (dot(own, edge_in[1]) + bias[0:1, :]).astype(BF16)
    spread = (
        lax.broadcasted_iota(jnp.int32, (count, nodes), 0) // DEG
        == lax.broadcasted_iota(jnp.int32, (count, nodes), 1)
    ).astype(F32).astype(BF16)
    picked = one_hot_rows(send_ref[...], nodes)
    pre_ref[...] = dot(edge_ref[...], edge_in[2]) + (dot(spread, receiver) + dot(picked, proj_ref[...]))
    own_ref[...] = dot(own, node_in[0]) + bias[2:3, :]
    w_ref[0] = centred_weight(edge_out[...])
    w_ref[1] = centred_weight(node_out[...])


def coarse_edge_terms(send, edges, nodes, proj, edge_in, edge_out, node_in, node_out, bias):
    shape = jax.ShapeDtypeStruct
    return pl.pallas_call(
        coarse_edges_kernel,
        out_shape=(shape(edges.shape, F32), shape(nodes.shape, F32), shape((2, 256, 256), BF16)),
        in_specs=[VMEM_SPEC] * 9,
        out_specs=(VMEM_SPEC,) * 3,
        cost_estimate=pl.CostEstimate(flops=500_000_000, bytes_accessed=3_000_000, transcendentals=0),
        name="coarse_edge_terms",
        compiler_params=limit(16),
    )(send, edges, nodes, proj, edge_in, edge_out, node_in, node_out, bias)


def coarse_kernel(send_ref, pre_ref, own_ref, w_ref, node_ref, low_ref, high_ref, node_in, bias, gain, out_ref):
    nodes = node_ref.shape[0]
    rim = low_ref.shape[0]
    count = pre_ref.shape[0]
    rims = jnp.concatenate([low_ref[...], high_ref[...]], axis=0)
    b_message = centred_row(bias[1:2, :])
    b_update = centred_row(bias[3:4, :])
    tnodes = TILE // DEG
    collect = (
        lax.broadcasted_iota(jnp.int32, (tnodes, TILE), 1) // DEG
        == lax.broadcasted_iota(jnp.int32, (tnodes, TILE), 0)
    ).astype(F32).astype(BF16)
    picked = one_hot_rows(send_ref[...] - nodes, 2 * rim)
    hidden = jnp.maximum(pre_ref[...] + dot(picked, rims), 0.0).astype(BF16)
    m = scaled_rows(dot(hidden, w_ref[0]) + b_message).astype(BF16)
    sums = [dot(collect, m[q : q + TILE, :]) for q in range(0, count, TILE)]
    summed = (jnp.concatenate(sums, axis=0) * gain[0:1, :]).astype(BF16)
    hidden = jnp.maximum(own_ref[...] + dot(summed, node_in[1]), 0.0).astype(BF16)
    u = scaled_rows(dot(hidden, w_ref[1]) + b_update) * gain[1:2, :]
    out_ref[...] = (node_ref[...].astype(F32) + u).astype(BF16)


def coarse_level(send, terms, nodes, low, high, node_in, bias, gain):
    pre, own, w = terms
    return pl.pallas_call(
        coarse_kernel,
        out_shape=jax.ShapeDtypeStruct(nodes.shape, BF16),
        in_specs=[VMEM_SPEC] * 10,
        out_specs=VMEM_SPEC,
        cost_estimate=pl.CostEstimate(flops=500_000_000, bytes_accessed=3_000_000, transcendentals=0),
        name="coarse_level",
        compiler_params=limit(16),
    )(send, pre, own, w, nodes, low, high, node_in, bias, gain)


def pair_swaps():
    count = lax.axis_size("dom")
    inner = [(i, i ^ 1) for i in range(count)]
    outer = [(i, ((i + 1) ^ 1) - 1) for i in range(1, count - 1)]
    return inner, outer


def body(
    node_lat,
    edge_lat,
    edge_send,
    halo_list,
    pool_id,
    coarse_lat,
    cedge_lat,
    cedge_send,
    chalo_list,
    fine_edge_in,
    fine_edge_out,
    fine_node_in,
    fine_node_out,
    fine_bias,
    fine_gain,
    coarse_edge_in,
    coarse_edge_out,
    coarse_node_in,
    coarse_node_out,
    coarse_bias,
    coarse_gain,
):
    inner, outer = pair_swaps()
    odd = lax.rem(lax.axis_index("dom"), 2)
    rim = halo_list.shape[0] // 2

    def table_row(send, count, rim_rows):
        lower = jnp.where(odd == 1, count, count + rim_rows)
        upper = jnp.where(odd == 1, count + rim_rows, count)
        return jnp.where(
            send < rim_rows,
            send + lower,
            jnp.where(
                send < rim_rows + count, send - rim_rows, send - (rim_rows + count) + upper
            ),
        )

    border_b, node_near, edge_in_near = border_rows(halo_list, node_lat, fine_edge_in, rim)
    rim_b = lax.ppermute(border_b, "dom", outer)
    border_a = own_rows(halo_list, node_near, edge_in_near, rim)
    rim_a = lax.ppermute(border_a, "dom", inner)
    groups = lax.axis_size("group")
    *terms, table = edge_terms(
        edge_send.reshape(-1, 128),
        pool_id.reshape(1, -1),
        edge_lat,
        node_near,
        rim,
        groups,
        edge_in_near,
        fine_edge_out,
        fine_node_in,
        fine_node_out,
        fine_bias,
    )
    fine_out, fine_near, far_up, far_down = fine_level(
        terms, table, node_near, rim_a, rim_b, fine_node_in, fine_bias, fine_gain
    )
    onward = [(i, (i + 1) % groups) for i in range(groups)]
    back = [(target, source) for source, target in onward]
    far_up = lax.ppermute(far_up, "group", onward)
    far_down = lax.ppermute(far_down, "group", back)
    next_rows, prev_rows, mine = pool_rows(terms[4], terms[5], fine_near)
    next_rows, prev_rows = relay_rows(next_rows, prev_rows, far_up, far_down)
    below = lax.ppermute(next_rows, "group", onward)
    above = lax.ppermute(prev_rows, "group", back)
    crim = chalo_list.shape[0] // 2
    clusters = coarse_lat.shape[0]
    lists = jnp.where(odd == 1, chalo_list, jnp.roll(chalo_list, crim))
    coarse_in, coarse_proj, cborder_a, cborder_b = cluster_level(
        mine, below, above, coarse_lat, lists.reshape(-1, 1), coarse_edge_in
    )
    crim_b = lax.ppermute(cborder_b, "dom", outer)
    crim_a = lax.ppermute(cborder_a, "dom", inner)
    csend = table_row(cedge_send, clusters, crim).reshape(-1, 1)
    cterms = coarse_edge_terms(
        csend,
        cedge_lat,
        coarse_in,
        coarse_proj,
        coarse_edge_in,
        coarse_edge_out,
        coarse_node_in,
        coarse_node_out,
        coarse_bias,
    )
    coarse_out = coarse_level(
        csend, cterms, coarse_in, crim_a, crim_b, coarse_node_in, coarse_bias, coarse_gain
    )
    return (fine_out, coarse_out)


def solution(mesh):
    rows = P(("group", "dom"), None)
    flat = P(("group", "dom"))
    placed = (rows, rows, flat, flat, flat, rows, rows, flat, flat) + (P(),) * 12

    return jax.shard_map(
        body,
        mesh=mesh,
        in_specs=placed,
        out_specs=(rows, rows),
        check_vma=False,
    )
```

```python
import jax
import jax.numpy as jnp
from jax import lax
from jax.experimental import pallas as pl
from jax.experimental.pallas import tpu as pltpu
from jax.sharding import PartitionSpec as P

EPSILON = 1e-05
F32 = jnp.float32
BF16 = jnp.bfloat16
CHUNK = 1024
GATHER = 2048
TILE = 256
DEG = 4
PIECE = 512

VMEM_SPEC = pl.BlockSpec(memory_space=pltpu.VMEM)
HBM_SPEC = pl.BlockSpec(memory_space=pltpu.HBM)


def hbm(x):
    return pltpu.with_memory_space_constraint(x, pltpu.HBM)


def limit(mib):
    return pltpu.CompilerParams(vmem_limit_bytes=mib * 1024 * 1024)


def dot(a, b):
    return jnp.dot(a, b, preferred_element_type=F32)


def centred_weight(w):
    w = w.astype(F32)
    return (w - jnp.mean(w, axis=-1, keepdims=True)).astype(BF16)


def centred_row(b):
    return b - jnp.mean(b, axis=-1, keepdims=True)


def scaled_rows(z):
    mean_square = jnp.mean(z * z, axis=-1, keepdims=True)
    return z * lax.rsqrt(mean_square + EPSILON)


def store_split(table, row, values):
    n = values.shape[0]
    table[pl.ds(2 * row, n, stride=2), :] = values[:, :128]
    table[pl.ds(2 * row + 1, n, stride=2), :] = values[:, 128:]


def load_split(table, row, n):
    return jnp.concatenate(
        [table[pl.ds(2 * row, n, stride=2), :], table[pl.ds(2 * row + 1, n, stride=2), :]],
        axis=1,
    )


def copy_rows(table, rows, index, count):
    for u in range(count):
        row = pl.multiple_of(index[u] * 2, 2)
        rows[2 * u : 2 * u + 2, :] = table[pl.ds(row, 2), :]


def border_kernel(
    list_ref, node_ref, w_ref, b_ref, nodes, w, table, rows, index, list_sem, w_sem, node_sem
):
    rim = b_ref.shape[0]
    odd = lax.rem(lax.axis_index("dom"), 2)
    copies = [
        pltpu.make_async_copy(node_ref.at[i : i + TILE, :], nodes.at[i : i + TILE, :], node_sem.at[i // TILE])
        for i in range(0, nodes.shape[0], TILE)
    ]
    for c in copies:
        c.start()
    first = pl.multiple_of(odd * rim, rim)
    list_copy = pltpu.make_async_copy(list_ref.at[pl.ds(first, rim)], index, list_sem)
    list_copy.start()
    w_copy = pltpu.make_async_copy(w_ref, w, w_sem)
    w_copy.start()
    for i, c in enumerate(copies):
        c.wait()
        store_split(table, i * TILE, nodes[i * TILE : (i + 1) * TILE, :].astype(F32))
    list_copy.wait()
    copy_rows(table, rows, index, rim)
    w_copy.wait()
    b_ref[...] = dot(load_split(rows, 0, rim).astype(BF16), w[0]).astype(BF16)


def border_rows(lists, nodes, edge_in, rim):
    shape = jax.ShapeDtypeStruct
    return pl.pallas_call(
        border_kernel,
        out_shape=(
            shape((rim, 256), BF16),
            shape(nodes.shape, BF16),
            shape(edge_in.shape, BF16),
        ),
        in_specs=[HBM_SPEC] * 3,
        out_specs=(VMEM_SPEC,) * 3,
        scratch_shapes=[
            pltpu.VMEM((2 * nodes.shape[0], 128), F32),
            pltpu.VMEM((2 * rim, 128), F32),
            pltpu.SMEM((rim,), jnp.int32),
            pltpu.SemaphoreType.DMA,
            pltpu.SemaphoreType.DMA,
            pltpu.SemaphoreType.DMA((nodes.shape[0] // TILE,)),
        ],
        cost_estimate=pl.CostEstimate(flops=70_000_000, bytes_accessed=2_000_000, transcendentals=0),
        name="border_rows",
        compiler_params=limit(8),
    )(hbm(lists), hbm(nodes), hbm(edge_in))


def own_kernel(list_ref, node_ref, w_ref, a_ref, table, rows, index, list_sem):
    rim = a_ref.shape[0]
    odd = lax.rem(lax.axis_index("dom"), 2)
    first = pl.multiple_of((1 - odd) * rim, rim)
    list_copy = pltpu.make_async_copy(list_ref.at[pl.ds(first, rim)], index, list_sem)
    list_copy.start()
    store_split(table, 0, node_ref[...].astype(F32))
    list_copy.wait()
    copy_rows(table, rows, index, rim)
    a_ref[...] = dot(load_split(rows, 0, rim).astype(BF16), w_ref[0]).astype(BF16)


def own_rows(lists, nodes, edge_in, rim):
    return pl.pallas_call(
        own_kernel,
        out_shape=jax.ShapeDtypeStruct((rim, 256), BF16),
        in_specs=[HBM_SPEC] + [VMEM_SPEC] * 2,
        out_specs=VMEM_SPEC,
        scratch_shapes=[
            pltpu.VMEM((2 * nodes.shape[0], 128), F32),
            pltpu.VMEM((2 * rim, 128), F32),
            pltpu.SMEM((rim,), jnp.int32),
            pltpu.SemaphoreType.DMA,
        ],
        cost_estimate=pl.CostEstimate(flops=70_000_000, bytes_accessed=2_000_000, transcendentals=0),
        name="own_rows",
        compiler_params=limit(8),
    )(hbm(lists), nodes, edge_in)


def membership(pool, step, member_ref, k, count_ref, at):
    nodes = pool.shape[1]
    owner = lax.rem(lax.axis_index("group") + step, lax.axis_size("group"))
    row = lax.broadcasted_iota(jnp.int32, (256, 128), 0).astype(F32).astype(BF16)
    lane = lax.broadcasted_iota(jnp.int32, (256, 128), 1)
    one = jnp.ones((256, 128), BF16)
    zero = jnp.zeros((256, 128), BF16)
    local = pool[...] - owner * 256
    inside = jnp.logical_and(local >= 0, local < 256)
    local = jnp.where(inside, local, 256).astype(F32).astype(BF16)
    total = zero
    for i in range(0, nodes, 128):
        here = jnp.broadcast_to(local[:, i : i + 128], (256, 128))
        member = jnp.where(row == here, one, zero)
        member_ref[k, :, i : i + 128] = member
        total = total + member
    count = jnp.sum(total.astype(F32), axis=1, keepdims=True)
    high = jnp.floor(count * (1.0 / 64.0))
    low = count - high * 64.0
    both = jnp.where(lane == 0, low, jnp.where(lane == 1, high, 0.0))
    count_ref[at] = both.T[:16, :].astype(BF16)


def edges_kernel(
    node,
    edge_in,
    send_hbm,
    pool_hbm,
    edge_out_hbm,
    node_in_hbm,
    node_out_hbm,
    bias_hbm,
    edge_hbm,
    pre_ref,
    own_ref,
    row_ref,
    w_ref,
    member_ref,
    count_ref,
    table_ref,
    send,
    pool,
    edge_out,
    node_in,
    node_out,
    bias,
    edges,
    rep0,
    rep1,
    rep2,
    rep3,
    small_sem,
    edge_sem,
):
    nodes = node.shape[0]
    chunks = edges.shape[0] // CHUNK
    cnodes = CHUNK // DEG
    rim = (table_ref.shape[0] // 2 - nodes) // 2
    small = [
        pltpu.make_async_copy(source, target, small_sem.at[i])
        for i, (source, target) in enumerate(
            (
                (bias_hbm, bias),
                (pool_hbm, pool),
                (send_hbm, send),
                (edge_out_hbm, edge_out),
                (node_in_hbm, node_in),
                (node_out_hbm, node_out),
            )
        )
    ]
    copies = [
        pltpu.make_async_copy(
            edge_hbm.at[c * CHUNK : (c + 1) * CHUNK, :],
            edges.at[c * CHUNK : (c + 1) * CHUNK, :],
            edge_sem.at[c],
        )
        for c in range(chunks)
    ]
    for c in small + copies:
        c.start()
    small[0].wait()
    small[1].wait()

    membership(pool, 2, member_ref, 0, count_ref, 0)
    b_edge = bias[0:1, :]
    b_node = bias[2:3, :]

    reps = ((rep0, rep1), (rep2, rep3))

    def spread(c, pair):
        c = jnp.minimum(c, chunks - 1)
        own = node[pl.ds(pl.multiple_of(c * cnodes, cnodes), cnodes), :]
        receiver = dot(own, edge_in[1]) + b_edge
        for half, rep in enumerate(pair):
            for j in range(DEG):
                rep[pl.ds(j, cnodes, stride=DEG), :] = receiver[:, 128 * half : 128 * half + 128]

    spread(0, reps[0])

    def edge_pair(k, carry):
        for slot in range(2):
            c = 2 * k + slot
            at = pl.ds(pl.multiple_of(c * CHUNK, CHUNK), CHUNK)
            pltpu.make_async_copy(edge_hbm.at[at, :], edges.at[at, :], edge_sem.at[c]).wait()
            spread(c + 1, reps[1 - slot])
            here = reps[slot]
            for i in range(0, CHUNK, PIECE):
                at = pl.ds(pl.multiple_of(c * CHUNK + i, PIECE), PIECE)
                near = [rep[i : i + PIECE, :] for rep in here]
                pre_ref[at, :] = dot(edges[at, :], edge_in[2]) + jnp.concatenate(near, axis=1)
        return carry

    lax.fori_loop(0, chunks // 2, edge_pair, 0)

    for c in small[2:]:
        c.wait()
    odd = lax.rem(lax.axis_index("dom"), 2)
    sent = send[...]
    lower = jnp.where(odd == 1, nodes, nodes + rim)
    upper = jnp.where(odd == 1, nodes + rim, nodes) - (rim + nodes)
    row_ref[...] = 2 * (
        sent + jnp.where(sent < rim, lower, jnp.where(sent < rim + nodes, -rim, upper))
    )
    w_ref[0] = centred_weight(edge_out[...])
    w_ref[1] = centred_weight(node_out[...])
    for i in range(0, nodes, CHUNK):
        own = node[i : i + CHUNK, :]
        store_split(table_ref, i, dot(own, edge_in[0]).astype(BF16).astype(F32))
        own_ref[i : i + CHUNK, :] = dot(own, node_in[0]) + b_node


def edge_terms(send, pool, edges, nodes, rim, edge_in, edge_out, node_in, node_out, bias):
    n = nodes.shape[0]
    e = edges.shape[0]
    shape = jax.ShapeDtypeStruct
    operands = (send, pool, edge_out, node_in, node_out, bias, edges)
    return pl.pallas_call(
        edges_kernel,
        out_shape=(
            shape((e, 256), F32),
            shape((n, 256), F32),
            shape(send.shape, jnp.int32),
            shape((2, 256, 256), BF16),
            shape((1, 256, n), BF16),
            shape((1, 16, 256), BF16),
            shape((2 * (n + 2 * rim), 128), F32),
        ),
        in_specs=[VMEM_SPEC] * 2 + [HBM_SPEC] * len(operands),
        out_specs=(VMEM_SPEC,) * 7,
        scratch_shapes=[pltpu.VMEM(x.shape, x.dtype) for x in operands]
        + [
            pltpu.VMEM((CHUNK, 128), F32),
            pltpu.VMEM((CHUNK, 128), F32),
            pltpu.VMEM((CHUNK, 128), F32),
            pltpu.VMEM((CHUNK, 128), F32),
            pltpu.SemaphoreType.DMA((6,)),
            pltpu.SemaphoreType.DMA((e // CHUNK,)),
        ],
        cost_estimate=pl.CostEstimate(flops=3_000_000_000, bytes_accessed=8_000_000, transcendentals=0),
        name="edge_terms",
        compiler_params=limit(14),
    )(nodes, edge_in, *(hbm(x) for x in operands))


def fine_kernel(
    row_ref,
    pre_ref,
    own_ref,
    table_ref,
    w_ref,
    member_ref,
    count_ref,
    low_ref,
    high_ref,
    node,
    node_in,
    bias,
    gain,
    out_hbm,
    out,
    up_ref,
    down_ref,
    table,
    rows,
    summed,
    index0,
    index1,
    index_sem,
    out_sem,
):
    nodes = node.shape[0]
    chunks = pre_ref.shape[0] // GATHER
    rim = low_ref.shape[0]
    cnodes = GATHER // DEG
    lines = GATHER // 128

    def index_copy(c, slot):
        c = jnp.minimum(c, chunks - 1)
        at = pl.ds(pl.multiple_of(c * lines, lines), lines)
        return pltpu.make_async_copy(
            row_ref.at[at, :], index1 if slot else index0, index_sem.at[slot]
        )

    index_copy(0, 0).start()
    index_copy(1, 1).start()
    store_split(table, nodes, low_ref[...].astype(F32))
    store_split(table, nodes + rim, high_ref[...].astype(F32))
    b_message = centred_row(bias[1:2, :])
    b_update = centred_row(bias[3:4, :])
    g_message = gain[0:1, :]
    g_update = gain[1:2, :]
    tnodes = TILE // DEG
    collect = (
        lax.broadcasted_iota(jnp.int32, (tnodes, TILE), 1) // DEG
        == lax.broadcasted_iota(jnp.int32, (tnodes, TILE), 0)
    ).astype(F32).astype(BF16)

    def pair(k, carry):
        for slot, index in enumerate((index0, index1)):
            c = 2 * k + slot
            index_copy(c, slot).wait()
            for u in range(GATHER):
                row = pl.multiple_of(index[u // 128, u % 128], 2)
                rows[2 * u : 2 * u + 2, :] = table[pl.ds(row, 2), :]
            index_copy(c + 2, slot).start()
            pre = pre_ref[pl.ds(pl.multiple_of(c * GATHER, GATHER), GATHER), :]
            hidden = jnp.maximum(pre + load_split(rows, 0, GATHER), 0.0).astype(BF16)
            m = scaled_rows(dot(hidden, w_ref[0]) + b_message).astype(BF16)
            sums = [dot(collect, m[q : q + TILE, :]) for q in range(0, GATHER, TILE)]
            summed[pl.ds(pl.multiple_of(c * cnodes, cnodes), cnodes), :] = (
                jnp.concatenate(sums, axis=0) * g_message
            ).astype(BF16)
        return carry

    lax.fori_loop(0, chunks // 2, pair, 0)
    index_copy(0, 0).wait()
    index_copy(1, 1).wait()
    hidden = jnp.maximum(own_ref[...] + dot(summed[...], node_in[1]), 0.0).astype(BF16)
    u = scaled_rows(dot(hidden, w_ref[1]) + b_update) * g_update
    out[...] = (node[...].astype(F32) + u).astype(BF16)
    out_copy = pltpu.make_async_copy(out, out_hbm, out_sem)
    out_copy.start()
    far = dot(member_ref[0], out[...]).astype(BF16)
    up_ref[:256, :] = far[:, :128]
    down_ref[:256, :] = far[:, 128:]
    up_ref[256:, :] = count_ref[0, :, :128]
    down_ref[256:, :] = count_ref[0, :, 128:]
    out_copy.wait()


def fine_level(terms, table, nodes, low, high, node_in, bias, gain):
    n = nodes.shape[0]
    pre, own, row, w, member, count = terms
    shape = jax.ShapeDtypeStruct
    outs = pl.pallas_call(
        fine_kernel,
        out_shape=(
            shape((n, 256), BF16),
            shape((n, 256), BF16),
            shape((272, 128), BF16),
            shape((272, 128), BF16),
            shape(table.shape, F32),
        ),
        in_specs=[VMEM_SPEC] * 13,
        out_specs=(HBM_SPEC,) + (VMEM_SPEC,) * 4,
        scratch_shapes=[
            pltpu.VMEM((2 * GATHER, 128), F32),
            pltpu.VMEM((n, 256), BF16),
            pltpu.SMEM((GATHER // 128, 128), jnp.int32),
            pltpu.SMEM((GATHER // 128, 128), jnp.int32),
            pltpu.SemaphoreType.DMA((2,)),
            pltpu.SemaphoreType.DMA,
        ],
        input_output_aliases={3: 4},
        cost_estimate=pl.CostEstimate(flops=4_000_000_000, bytes_accessed=8_000_000, transcendentals=0),
        name="fine_level",
        compiler_params=pltpu.CompilerParams(vmem_limit_bytes=14 * 1024 * 1024),
    )(row, pre, own, table, w, member, count, low, high, nodes, node_in, bias, gain)
    return outs[:4]


def pool_kernel(pool, out_ref, next_ref, prev_ref, mine_ref, member, count):
    for k, (step, ref) in enumerate(((1, next_ref), (3, prev_ref), (0, mine_ref))):
        membership(pool, step, member, k, count, k)
        ref[:256, :] = dot(member[k], out_ref[...]).astype(BF16)
        ref[256:, :] = count[k]


def pool_rows(pool, out):
    shape = jax.ShapeDtypeStruct((272, 256), BF16)
    return pl.pallas_call(
        pool_kernel,
        out_shape=(shape,) * 3,
        in_specs=[VMEM_SPEC] * 2,
        out_specs=(VMEM_SPEC,) * 3,
        scratch_shapes=[
            pltpu.VMEM((3, 256, out.shape[0]), BF16),
            pltpu.VMEM((3, 16, 256), BF16),
        ],
        cost_estimate=pl.CostEstimate(flops=800_000_000, bytes_accessed=4_000_000, transcendentals=0),
        name="pool_rows",
        compiler_params=limit(10),
    )(pool, out)


def relay_kernel(next_ref, prev_ref, up_ref, down_ref, next_out, prev_out):
    next_out[:, :128] = (next_ref[:, :128].astype(F32) + up_ref[...].astype(F32)).astype(BF16)
    next_out[:, 128:] = next_ref[:, 128:]
    prev_out[:, :128] = prev_ref[:, :128]
    prev_out[:, 128:] = (prev_ref[:, 128:].astype(F32) + down_ref[...].astype(F32)).astype(BF16)


def relay_rows(next_rows, prev_rows, up, down):
    shape = jax.ShapeDtypeStruct((272, 256), BF16)
    return pl.pallas_call(
        relay_kernel,
        out_shape=(shape,) * 2,
        in_specs=[VMEM_SPEC] * 4,
        out_specs=(VMEM_SPEC,) * 2,
        cost_estimate=pl.CostEstimate(flops=200_000, bytes_accessed=1_000_000, transcendentals=0),
        name="relay_rows",
        compiler_params=limit(8),
    )(next_rows, prev_rows, up, down)


def one_hot_rows(index_col, count):
    return (
        index_col == lax.broadcasted_iota(jnp.int32, (index_col.shape[0], count), 1)
    ).astype(F32).astype(BF16)


def cluster_kernel(mine_ref, below_ref, above_ref, lat_ref, list_ref, w_ref, in_ref, proj_ref, a_ref, b_ref):
    clusters = lat_ref.shape[0]
    rim = a_ref.shape[0]
    total = mine_ref[...].astype(F32) + below_ref[...].astype(F32) + above_ref[...].astype(F32)
    count = total[clusters : clusters + 1, :] + 64.0 * total[clusters + 1 : clusters + 2, :]
    total = total[:clusters, :]
    count = jnp.broadcast_to(count, (8, clusters)).T[:, :1]
    mean = total / jnp.maximum(count, 1.0)
    coarse_in = (lat_ref[...].astype(F32) + mean).astype(BF16)
    in_ref[...] = coarse_in
    proj = dot(coarse_in, w_ref[0]).astype(BF16)
    proj_ref[...] = proj
    border = dot(one_hot_rows(list_ref[...], clusters), proj)
    low, high = border[:rim, :], border[rim:, :]
    odd = lax.rem(lax.axis_index("dom"), 2) == 1
    a_ref[...] = jnp.where(odd, low, high).astype(BF16)
    b_ref[...] = jnp.where(odd, high, low).astype(BF16)


def cluster_level(mine, below, above, lat, lists, edge_in):
    n = lat.shape[0]
    shape = jax.ShapeDtypeStruct((n, 256), BF16)
    rim = jax.ShapeDtypeStruct((lists.shape[0] // 2, 256), BF16)
    return pl.pallas_call(
        cluster_kernel,
        out_shape=(shape, shape, rim, rim),
        in_specs=[VMEM_SPEC] * 6,
        out_specs=(VMEM_SPEC,) * 4,
        cost_estimate=pl.CostEstimate(flops=70_000_000, bytes_accessed=1_000_000, transcendentals=0),
        name="cluster_level",
        compiler_params=limit(16),
    )(mine, below, above, lat, lists, edge_in)


def coarse_edges_kernel(send_ref, edge_ref, node_ref, proj_ref, edge_in, edge_out, node_in, node_out, bias, pre_ref, own_ref, w_ref):
    nodes = node_ref.shape[0]
    count = edge_ref.shape[0]
    own = node_ref[...]
    receiver = (dot(own, edge_in[1]) + bias[0:1, :]).astype(BF16)
    spread = (
        lax.broadcasted_iota(jnp.int32, (count, nodes), 0) // DEG
        == lax.broadcasted_iota(jnp.int32, (count, nodes), 1)
    ).astype(F32).astype(BF16)
    picked = one_hot_rows(send_ref[...], nodes)
    pre_ref[...] = dot(edge_ref[...], edge_in[2]) + (dot(spread, receiver) + dot(picked, proj_ref[...]))
    own_ref[...] = dot(own, node_in[0]) + bias[2:3, :]
    w_ref[0] = centred_weight(edge_out[...])
    w_ref[1] = centred_weight(node_out[...])


def coarse_edge_terms(send, edges, nodes, proj, edge_in, edge_out, node_in, node_out, bias):
    shape = jax.ShapeDtypeStruct
    return pl.pallas_call(
        coarse_edges_kernel,
        out_shape=(shape(edges.shape, F32), shape(nodes.shape, F32), shape((2, 256, 256), BF16)),
        in_specs=[VMEM_SPEC] * 9,
        out_specs=(VMEM_SPEC,) * 3,
        cost_estimate=pl.CostEstimate(flops=500_000_000, bytes_accessed=3_000_000, transcendentals=0),
        name="coarse_edge_terms",
        compiler_params=limit(16),
    )(send, edges, nodes, proj, edge_in, edge_out, node_in, node_out, bias)


def coarse_kernel(send_ref, pre_ref, own_ref, w_ref, node_ref, low_ref, high_ref, node_in, bias, gain, out_ref):
    nodes = node_ref.shape[0]
    rim = low_ref.shape[0]
    count = pre_ref.shape[0]
    rims = jnp.concatenate([low_ref[...], high_ref[...]], axis=0)
    b_message = centred_row(bias[1:2, :])
    b_update = centred_row(bias[3:4, :])
    tnodes = TILE // DEG
    collect = (
        lax.broadcasted_iota(jnp.int32, (tnodes, TILE), 1) // DEG
        == lax.broadcasted_iota(jnp.int32, (tnodes, TILE), 0)
    ).astype(F32).astype(BF16)
    picked = one_hot_rows(send_ref[...] - nodes, 2 * rim)
    hidden = jnp.maximum(pre_ref[...] + dot(picked, rims), 0.0).astype(BF16)
    m = scaled_rows(dot(hidden, w_ref[0]) + b_message).astype(BF16)
    sums = [dot(collect, m[q : q + TILE, :]) for q in range(0, count, TILE)]
    summed = (jnp.concatenate(sums, axis=0) * gain[0:1, :]).astype(BF16)
    hidden = jnp.maximum(own_ref[...] + dot(summed, node_in[1]), 0.0).astype(BF16)
    u = scaled_rows(dot(hidden, w_ref[1]) + b_update) * gain[1:2, :]
    out_ref[...] = (node_ref[...].astype(F32) + u).astype(BF16)


def coarse_level(send, terms, nodes, low, high, node_in, bias, gain):
    pre, own, w = terms
    return pl.pallas_call(
        coarse_kernel,
        out_shape=jax.ShapeDtypeStruct(nodes.shape, BF16),
        in_specs=[VMEM_SPEC] * 10,
        out_specs=VMEM_SPEC,
        cost_estimate=pl.CostEstimate(flops=500_000_000, bytes_accessed=3_000_000, transcendentals=0),
        name="coarse_level",
        compiler_params=limit(16),
    )(send, pre, own, w, nodes, low, high, node_in, bias, gain)


def pair_swaps():
    count = lax.axis_size("dom")
    inner = [(i, i ^ 1) for i in range(count)]
    outer = [(i, ((i + 1) ^ 1) - 1) for i in range(1, count - 1)]
    return inner, outer


def body(
    node_lat,
    edge_lat,
    edge_send,
    halo_list,
    pool_id,
    coarse_lat,
    cedge_lat,
    cedge_send,
    chalo_list,
    fine_edge_in,
    fine_edge_out,
    fine_node_in,
    fine_node_out,
    fine_bias,
    fine_gain,
    coarse_edge_in,
    coarse_edge_out,
    coarse_node_in,
    coarse_node_out,
    coarse_bias,
    coarse_gain,
):
    inner, outer = pair_swaps()
    odd = lax.rem(lax.axis_index("dom"), 2)
    rim = halo_list.shape[0] // 2

    def table_row(send, count, rim_rows):
        lower = jnp.where(odd == 1, count, count + rim_rows)
        upper = jnp.where(odd == 1, count + rim_rows, count)
        return jnp.where(
            send < rim_rows,
            send + lower,
            jnp.where(
                send < rim_rows + count, send - rim_rows, send - (rim_rows + count) + upper
            ),
        )

    border_b, node_near, edge_in_near = border_rows(halo_list, node_lat, fine_edge_in, rim)
    rim_b = lax.ppermute(border_b, "dom", outer)
    border_a = own_rows(halo_list, node_near, edge_in_near, rim)
    rim_a = lax.ppermute(border_a, "dom", inner)
    groups = lax.axis_size("group")
    *terms, table = edge_terms(
        edge_send.reshape(-1, 128),
        pool_id.reshape(1, -1),
        edge_lat,
        node_near,
        rim,
        edge_in_near,
        fine_edge_out,
        fine_node_in,
        fine_node_out,
        fine_bias,
    )
    fine_out, fine_near, far_up, far_down = fine_level(
        terms, table, node_near, rim_a, rim_b, fine_node_in, fine_bias, fine_gain
    )
    onward = [(i, (i + 1) % groups) for i in range(groups)]
    back = [(target, source) for source, target in onward]
    far_up = lax.ppermute(far_up, "group", onward)
    far_down = lax.ppermute(far_down, "group", back)
    next_rows, prev_rows, mine = pool_rows(pool_id.reshape(1, -1), fine_near)
    next_rows, prev_rows = relay_rows(next_rows, prev_rows, far_up, far_down)
    below = lax.ppermute(next_rows, "group", onward)
    above = lax.ppermute(prev_rows, "group", back)
    crim = chalo_list.shape[0] // 2
    clusters = coarse_lat.shape[0]
    coarse_in, coarse_proj, cborder_a, cborder_b = cluster_level(
        mine, below, above, coarse_lat, chalo_list.reshape(-1, 1), coarse_edge_in
    )
    crim_b = lax.ppermute(cborder_b, "dom", outer)
    crim_a = lax.ppermute(cborder_a, "dom", inner)
    csend = table_row(cedge_send, clusters, crim).reshape(-1, 1)
    cterms = coarse_edge_terms(
        csend,
        cedge_lat,
        coarse_in,
        coarse_proj,
        coarse_edge_in,
        coarse_edge_out,
        coarse_node_in,
        coarse_node_out,
        coarse_bias,
    )
    coarse_out = coarse_level(
        csend, cterms, coarse_in, crim_a, crim_b, coarse_node_in, coarse_bias, coarse_gain
    )
    return (fine_out, coarse_out)


def solution(mesh):
    rows = P(("group", "dom"), None)
    flat = P(("group", "dom"))
    placed = (rows, rows, flat, flat, flat, rows, rows, flat, flat) + (P(),) * 12

    return jax.shard_map(
        body,
        mesh=mesh,
        in_specs=placed,
        out_specs=(rows, rows),
        check_vma=False,
    )
```

```python
import jax
import jax.numpy as jnp
from jax import lax
from jax.experimental import pallas as pl
from jax.experimental.pallas import tpu as pltpu
from jax.sharding import PartitionSpec as P

EPSILON = 1e-05
F32 = jnp.float32
BF16 = jnp.bfloat16
CHUNK = 1024
GATHER = 2048
TILE = 256
DEG = 4
PIECE = 512

VMEM_SPEC = pl.BlockSpec(memory_space=pltpu.VMEM)
HBM_SPEC = pl.BlockSpec(memory_space=pltpu.HBM)


def hbm(x):
    return pltpu.with_memory_space_constraint(x, pltpu.HBM)


def limit(mib):
    return pltpu.CompilerParams(vmem_limit_bytes=mib * 1024 * 1024)


def dot(a, b):
    return jnp.dot(a, b, preferred_element_type=F32)


def centred_weight(w):
    w = w.astype(F32)
    return (w - jnp.mean(w, axis=-1, keepdims=True)).astype(BF16)


def centred_row(b):
    return b - jnp.mean(b, axis=-1, keepdims=True)


def scaled_rows(z):
    mean_square = jnp.mean(z * z, axis=-1, keepdims=True)
    return z * lax.rsqrt(mean_square + EPSILON)


def store_split(table, row, values):
    n = values.shape[0]
    table[pl.ds(2 * row, n, stride=2), :] = values[:, :128]
    table[pl.ds(2 * row + 1, n, stride=2), :] = values[:, 128:]


def load_split(table, row, n):
    return jnp.concatenate(
        [table[pl.ds(2 * row, n, stride=2), :], table[pl.ds(2 * row + 1, n, stride=2), :]],
        axis=1,
    )


def copy_rows(table, rows, index, count):
    for u in range(count):
        row = pl.multiple_of(index[u] * 2, 2)
        rows[2 * u : 2 * u + 2, :] = table[pl.ds(row, 2), :]


def border_kernel(
    list_ref, node_ref, w_ref, b_ref, nodes, w, table, rows, index, list_sem, w_sem, node_sem
):
    rim = b_ref.shape[0]
    odd = lax.rem(lax.axis_index("dom"), 2)
    copies = [
        pltpu.make_async_copy(node_ref.at[i : i + TILE, :], nodes.at[i : i + TILE, :], node_sem.at[i // TILE])
        for i in range(0, nodes.shape[0], TILE)
    ]
    for c in copies:
        c.start()
    first = pl.multiple_of(odd * rim, rim)
    list_copy = pltpu.make_async_copy(list_ref.at[pl.ds(first, rim)], index, list_sem)
    list_copy.start()
    w_copy = pltpu.make_async_copy(w_ref, w, w_sem)
    w_copy.start()
    for i, c in enumerate(copies):
        c.wait()
        store_split(table, i * TILE, nodes[i * TILE : (i + 1) * TILE, :].astype(F32))
    list_copy.wait()
    copy_rows(table, rows, index, rim)
    w_copy.wait()
    b_ref[...] = dot(load_split(rows, 0, rim).astype(BF16), w[0]).astype(BF16)


def border_rows(lists, nodes, edge_in, rim):
    shape = jax.ShapeDtypeStruct
    return pl.pallas_call(
        border_kernel,
        out_shape=(
            shape((rim, 256), BF16),
            shape(nodes.shape, BF16),
            shape(edge_in.shape, BF16),
        ),
        in_specs=[HBM_SPEC] * 3,
        out_specs=(VMEM_SPEC,) * 3,
        scratch_shapes=[
            pltpu.VMEM((2 * nodes.shape[0], 128), F32),
            pltpu.VMEM((2 * rim, 128), F32),
            pltpu.SMEM((rim,), jnp.int32),
            pltpu.SemaphoreType.DMA,
            pltpu.SemaphoreType.DMA,
            pltpu.SemaphoreType.DMA((nodes.shape[0] // TILE,)),
        ],
        cost_estimate=pl.CostEstimate(flops=70_000_000, bytes_accessed=2_000_000, transcendentals=0),
        name="border_rows",
        compiler_params=limit(8),
    )(hbm(lists), hbm(nodes), hbm(edge_in))


def own_kernel(list_ref, node_ref, w_ref, a_ref, table, rows, index, list_sem):
    rim = a_ref.shape[0]
    odd = lax.rem(lax.axis_index("dom"), 2)
    first = pl.multiple_of((1 - odd) * rim, rim)
    list_copy = pltpu.make_async_copy(list_ref.at[pl.ds(first, rim)], index, list_sem)
    list_copy.start()
    store_split(table, 0, node_ref[...].astype(F32))
    list_copy.wait()
    copy_rows(table, rows, index, rim)
    a_ref[...] = dot(load_split(rows, 0, rim).astype(BF16), w_ref[0]).astype(BF16)


def own_rows(lists, nodes, edge_in, rim):
    return pl.pallas_call(
        own_kernel,
        out_shape=jax.ShapeDtypeStruct((rim, 256), BF16),
        in_specs=[HBM_SPEC] + [VMEM_SPEC] * 2,
        out_specs=VMEM_SPEC,
        scratch_shapes=[
            pltpu.VMEM((2 * nodes.shape[0], 128), F32),
            pltpu.VMEM((2 * rim, 128), F32),
            pltpu.SMEM((rim,), jnp.int32),
            pltpu.SemaphoreType.DMA,
        ],
        cost_estimate=pl.CostEstimate(flops=70_000_000, bytes_accessed=2_000_000, transcendentals=0),
        name="own_rows",
        compiler_params=limit(8),
    )(hbm(lists), nodes, edge_in)


def membership(pool, step, member_ref, k, count_ref, at):
    nodes = pool.shape[1]
    owner = lax.rem(lax.axis_index("group") + step, lax.axis_size("group"))
    row = lax.broadcasted_iota(jnp.int32, (256, 128), 0).astype(F32).astype(BF16)
    lane = lax.broadcasted_iota(jnp.int32, (256, 128), 1)
    one = jnp.ones((256, 128), BF16)
    zero = jnp.zeros((256, 128), BF16)
    local = pool[...] - owner * 256
    inside = jnp.logical_and(local >= 0, local < 256)
    local = jnp.where(inside, local, 256).astype(F32).astype(BF16)
    total = zero
    for i in range(0, nodes, 128):
        here = jnp.broadcast_to(local[:, i : i + 128], (256, 128))
        member = jnp.where(row == here, one, zero)
        member_ref[k, :, i : i + 128] = member
        total = total + member
    count = jnp.sum(total.astype(F32), axis=1, keepdims=True)
    high = jnp.floor(count * (1.0 / 64.0))
    low = count - high * 64.0
    both = jnp.where(lane == 0, low, jnp.where(lane == 1, high, 0.0))
    count_ref[at] = both.T[:16, :].astype(BF16)


def edges_kernel(
    node,
    edge_in,
    send_hbm,
    pool_hbm,
    edge_out_hbm,
    node_in_hbm,
    node_out_hbm,
    bias_hbm,
    edge_hbm,
    pre_ref,
    own_ref,
    row_ref,
    w_ref,
    member_ref,
    count_ref,
    table_ref,
    send,
    pool,
    edge_out,
    node_in,
    node_out,
    bias,
    edges,
    rep0,
    rep1,
    rep2,
    rep3,
    small_sem,
    edge_sem,
):
    nodes = node.shape[0]
    chunks = edges.shape[0] // CHUNK
    cnodes = CHUNK // DEG
    rim = (table_ref.shape[0] // 2 - nodes) // 2
    small = [
        pltpu.make_async_copy(source, target, small_sem.at[i])
        for i, (source, target) in enumerate(
            (
                (bias_hbm, bias),
                (pool_hbm, pool),
                (send_hbm, send),
                (edge_out_hbm, edge_out),
                (node_in_hbm, node_in),
                (node_out_hbm, node_out),
            )
        )
    ]
    copies = [
        pltpu.make_async_copy(
            edge_hbm.at[c * CHUNK : (c + 1) * CHUNK, :],
            edges.at[c * CHUNK : (c + 1) * CHUNK, :],
            edge_sem.at[c],
        )
        for c in range(chunks)
    ]
    for c in small + copies:
        c.start()
    small[0].wait()
    small[1].wait()

    membership(pool, 2, member_ref, 0, count_ref, 0)
    b_edge = bias[0:1, :]
    b_node = bias[2:3, :]

    reps = ((rep0, rep1), (rep2, rep3))

    def spread(c, pair):
        c = jnp.minimum(c, chunks - 1)
        own = node[pl.ds(pl.multiple_of(c * cnodes, cnodes), cnodes), :]
        receiver = dot(own, edge_in[1]) + b_edge
        for half, rep in enumerate(pair):
            for j in range(DEG):
                rep[pl.ds(j, cnodes, stride=DEG), :] = receiver[:, 128 * half : 128 * half + 128]

    spread(0, reps[0])

    def edge_pair(k, carry):
        for slot in range(2):
            c = 2 * k + slot
            at = pl.ds(pl.multiple_of(c * CHUNK, CHUNK), CHUNK)
            pltpu.make_async_copy(edge_hbm.at[at, :], edges.at[at, :], edge_sem.at[c]).wait()
            spread(c + 1, reps[1 - slot])
            here = reps[slot]
            for i in range(0, CHUNK, PIECE):
                at = pl.ds(pl.multiple_of(c * CHUNK + i, PIECE), PIECE)
                near = [rep[i : i + PIECE, :] for rep in here]
                pre_ref[at, :] = dot(edges[at, :], edge_in[2]) + jnp.concatenate(near, axis=1)
        return carry

    lax.fori_loop(0, chunks // 2, edge_pair, 0)

    for c in small[2:]:
        c.wait()
    odd = lax.rem(lax.axis_index("dom"), 2)
    sent = send[...]
    lower = jnp.where(odd == 1, nodes, nodes + rim)
    upper = jnp.where(odd == 1, nodes + rim, nodes) - (rim + nodes)
    row_ref[...] = 2 * (
        sent + jnp.where(sent < rim, lower, jnp.where(sent < rim + nodes, -rim, upper))
    )
    w_ref[0] = centred_weight(edge_out[...])
    w_ref[1] = centred_weight(node_out[...])
    for i in range(0, nodes, CHUNK):
        own = node[i : i + CHUNK, :]
        store_split(table_ref, i, dot(own, edge_in[0]).astype(BF16).astype(F32))
        own_ref[i : i + CHUNK, :] = dot(own, node_in[0]) + b_node


def edge_terms(send, pool, edges, nodes, rim, edge_in, edge_out, node_in, node_out, bias):
    n = nodes.shape[0]
    e = edges.shape[0]
    shape = jax.ShapeDtypeStruct
    operands = (send, pool, edge_out, node_in, node_out, bias, edges)
    return pl.pallas_call(
        edges_kernel,
        out_shape=(
            shape((e, 256), F32),
            shape((n, 256), F32),
            shape(send.shape, jnp.int32),
            shape((2, 256, 256), BF16),
            shape((1, 256, n), BF16),
            shape((1, 16, 256), BF16),
            shape((2 * (n + 2 * rim), 128), F32),
        ),
        in_specs=[VMEM_SPEC] * 2 + [HBM_SPEC] * len(operands),
        out_specs=(VMEM_SPEC,) * 7,
        scratch_shapes=[pltpu.VMEM(x.shape, x.dtype) for x in operands]
        + [
            pltpu.VMEM((CHUNK, 128), F32),
            pltpu.VMEM((CHUNK, 128), F32),
            pltpu.VMEM((CHUNK, 128), F32),
            pltpu.VMEM((CHUNK, 128), F32),
            pltpu.SemaphoreType.DMA((6,)),
            pltpu.SemaphoreType.DMA((e // CHUNK,)),
        ],
        cost_estimate=pl.CostEstimate(flops=3_000_000_000, bytes_accessed=8_000_000, transcendentals=0),
        name="edge_terms",
        compiler_params=limit(14),
    )(nodes, edge_in, *(hbm(x) for x in operands))


def fine_kernel(
    row_ref,
    pre_ref,
    own_ref,
    table_ref,
    w_ref,
    member_ref,
    count_ref,
    low_ref,
    high_ref,
    node,
    node_in,
    bias,
    gain,
    out,
    up_ref,
    down_ref,
    table,
    rows,
    summed,
    index0,
    index1,
    index_sem,
):
    nodes = node.shape[0]
    chunks = pre_ref.shape[0] // GATHER
    rim = low_ref.shape[0]
    cnodes = GATHER // DEG
    lines = GATHER // 128

    def index_copy(c, slot):
        c = jnp.minimum(c, chunks - 1)
        at = pl.ds(pl.multiple_of(c * lines, lines), lines)
        return pltpu.make_async_copy(
            row_ref.at[at, :], index1 if slot else index0, index_sem.at[slot]
        )

    index_copy(0, 0).start()
    index_copy(1, 1).start()
    store_split(table, nodes, low_ref[...].astype(F32))
    store_split(table, nodes + rim, high_ref[...].astype(F32))
    b_message = centred_row(bias[1:2, :])
    b_update = centred_row(bias[3:4, :])
    g_message = gain[0:1, :]
    g_update = gain[1:2, :]
    tnodes = TILE // DEG
    collect = (
        lax.broadcasted_iota(jnp.int32, (tnodes, TILE), 1) // DEG
        == lax.broadcasted_iota(jnp.int32, (tnodes, TILE), 0)
    ).astype(F32).astype(BF16)

    def pair(k, carry):
        for slot, index in enumerate((index0, index1)):
            c = 2 * k + slot
            index_copy(c, slot).wait()
            for u in range(GATHER):
                row = pl.multiple_of(index[u // 128, u % 128], 2)
                rows[2 * u : 2 * u + 2, :] = table[pl.ds(row, 2), :]
            index_copy(c + 2, slot).start()
            pre = pre_ref[pl.ds(pl.multiple_of(c * GATHER, GATHER), GATHER), :]
            hidden = jnp.maximum(pre + load_split(rows, 0, GATHER), 0.0).astype(BF16)
            m = scaled_rows(dot(hidden, w_ref[0]) + b_message).astype(BF16)
            sums = [dot(collect, m[q : q + TILE, :]) for q in range(0, GATHER, TILE)]
            summed[pl.ds(pl.multiple_of(c * cnodes, cnodes), cnodes), :] = (
                jnp.concatenate(sums, axis=0) * g_message
            ).astype(BF16)
        return carry

    lax.fori_loop(0, chunks // 2, pair, 0)
    index_copy(0, 0).wait()
    index_copy(1, 1).wait()
    hidden = jnp.maximum(own_ref[...] + dot(summed[...], node_in[1]), 0.0).astype(BF16)
    u = scaled_rows(dot(hidden, w_ref[1]) + b_update) * g_update
    out[...] = (node[...].astype(F32) + u).astype(BF16)
    far = dot(member_ref[0], out[...]).astype(BF16)
    up_ref[:256, :] = far[:, :128]
    down_ref[:256, :] = far[:, 128:]
    up_ref[256:, :] = count_ref[0, :, :128]
    down_ref[256:, :] = count_ref[0, :, 128:]


def fine_level(terms, table, nodes, low, high, node_in, bias, gain):
    n = nodes.shape[0]
    pre, own, row, w, member, count = terms
    shape = jax.ShapeDtypeStruct
    outs = pl.pallas_call(
        fine_kernel,
        out_shape=(
            shape((n, 256), BF16),
            shape((272, 128), BF16),
            shape((272, 128), BF16),
            shape(table.shape, F32),
        ),
        in_specs=[VMEM_SPEC] * 13,
        out_specs=(VMEM_SPEC,) * 4,
        scratch_shapes=[
            pltpu.VMEM((2 * GATHER, 128), F32),
            pltpu.VMEM((n, 256), BF16),
            pltpu.SMEM((GATHER // 128, 128), jnp.int32),
            pltpu.SMEM((GATHER // 128, 128), jnp.int32),
            pltpu.SemaphoreType.DMA((2,)),
        ],
        input_output_aliases={3: 3},
        cost_estimate=pl.CostEstimate(flops=4_000_000_000, bytes_accessed=8_000_000, transcendentals=0),
        name="fine_level",
        compiler_params=pltpu.CompilerParams(vmem_limit_bytes=14 * 1024 * 1024),
    )(row, pre, own, table, w, member, count, low, high, nodes, node_in, bias, gain)
    return outs[:3]


def pool_kernel(pool, out_ref, out_hbm, next_ref, prev_ref, mine_ref, member, count, sem):
    out_copy = pltpu.make_async_copy(out_ref, out_hbm, sem)
    out_copy.start()
    for k, (step, ref) in enumerate(((1, next_ref), (3, prev_ref), (0, mine_ref))):
        membership(pool, step, member, k, count, k)
        ref[:256, :] = dot(member[k], out_ref[...]).astype(BF16)
        ref[256:, :] = count[k]
    out_copy.wait()


def pool_rows(pool, out):
    shape = jax.ShapeDtypeStruct((272, 256), BF16)
    return pl.pallas_call(
        pool_kernel,
        out_shape=(jax.ShapeDtypeStruct(out.shape, BF16),) + (shape,) * 3,
        in_specs=[VMEM_SPEC] * 2,
        out_specs=(HBM_SPEC,) + (VMEM_SPEC,) * 3,
        scratch_shapes=[
            pltpu.VMEM((3, 256, out.shape[0]), BF16),
            pltpu.VMEM((3, 16, 256), BF16),
            pltpu.SemaphoreType.DMA,
        ],
        cost_estimate=pl.CostEstimate(flops=800_000_000, bytes_accessed=4_000_000, transcendentals=0),
        name="pool_rows",
        compiler_params=limit(10),
    )(pool, out)


def relay_kernel(next_ref, prev_ref, up_ref, down_ref, next_out, prev_out):
    next_out[:, :128] = (next_ref[:, :128].astype(F32) + up_ref[...].astype(F32)).astype(BF16)
    next_out[:, 128:] = next_ref[:, 128:]
    prev_out[:, :128] = prev_ref[:, :128]
    prev_out[:, 128:] = (prev_ref[:, 128:].astype(F32) + down_ref[...].astype(F32)).astype(BF16)


def relay_rows(next_rows, prev_rows, up, down):
    shape = jax.ShapeDtypeStruct((272, 256), BF16)
    return pl.pallas_call(
        relay_kernel,
        out_shape=(shape,) * 2,
        in_specs=[VMEM_SPEC] * 4,
        out_specs=(VMEM_SPEC,) * 2,
        cost_estimate=pl.CostEstimate(flops=200_000, bytes_accessed=1_000_000, transcendentals=0),
        name="relay_rows",
        compiler_params=limit(8),
    )(next_rows, prev_rows, up, down)


def one_hot_rows(index_col, count):
    return (
        index_col == lax.broadcasted_iota(jnp.int32, (index_col.shape[0], count), 1)
    ).astype(F32).astype(BF16)


def cluster_kernel(mine_ref, below_ref, above_ref, lat_ref, list_ref, w_ref, in_ref, proj_ref, a_ref, b_ref):
    clusters = lat_ref.shape[0]
    rim = a_ref.shape[0]
    total = mine_ref[...].astype(F32) + below_ref[...].astype(F32) + above_ref[...].astype(F32)
    count = total[clusters : clusters + 1, :] + 64.0 * total[clusters + 1 : clusters + 2, :]
    total = total[:clusters, :]
    count = jnp.broadcast_to(count, (8, clusters)).T[:, :1]
    mean = total / jnp.maximum(count, 1.0)
    coarse_in = (lat_ref[...].astype(F32) + mean).astype(BF16)
    in_ref[...] = coarse_in
    proj = dot(coarse_in, w_ref[0]).astype(BF16)
    proj_ref[...] = proj
    border = dot(one_hot_rows(list_ref[...], clusters), proj)
    low, high = border[:rim, :], border[rim:, :]
    odd = lax.rem(lax.axis_index("dom"), 2) == 1
    a_ref[...] = jnp.where(odd, low, high).astype(BF16)
    b_ref[...] = jnp.where(odd, high, low).astype(BF16)


def cluster_level(mine, below, above, lat, lists, edge_in):
    n = lat.shape[0]
    shape = jax.ShapeDtypeStruct((n, 256), BF16)
    rim = jax.ShapeDtypeStruct((lists.shape[0] // 2, 256), BF16)
    return pl.pallas_call(
        cluster_kernel,
        out_shape=(shape, shape, rim, rim),
        in_specs=[VMEM_SPEC] * 6,
        out_specs=(VMEM_SPEC,) * 4,
        cost_estimate=pl.CostEstimate(flops=70_000_000, bytes_accessed=1_000_000, transcendentals=0),
        name="cluster_level",
        compiler_params=limit(16),
    )(mine, below, above, lat, lists, edge_in)


def coarse_edges_kernel(send_ref, edge_ref, node_ref, proj_ref, edge_in, edge_out, node_in, node_out, bias, pre_ref, own_ref, w_ref):
    nodes = node_ref.shape[0]
    count = edge_ref.shape[0]
    own = node_ref[...]
    receiver = (dot(own, edge_in[1]) + bias[0:1, :]).astype(BF16)
    spread = (
        lax.broadcasted_iota(jnp.int32, (count, nodes), 0) // DEG
        == lax.broadcasted_iota(jnp.int32, (count, nodes), 1)
    ).astype(F32).astype(BF16)
    picked = one_hot_rows(send_ref[...], nodes)
    pre_ref[...] = dot(edge_ref[...], edge_in[2]) + (dot(spread, receiver) + dot(picked, proj_ref[...]))
    own_ref[...] = dot(own, node_in[0]) + bias[2:3, :]
    w_ref[0] = centred_weight(edge_out[...])
    w_ref[1] = centred_weight(node_out[...])


def coarse_edge_terms(send, edges, nodes, proj, edge_in, edge_out, node_in, node_out, bias):
    shape = jax.ShapeDtypeStruct
    return pl.pallas_call(
        coarse_edges_kernel,
        out_shape=(shape(edges.shape, F32), shape(nodes.shape, F32), shape((2, 256, 256), BF16)),
        in_specs=[VMEM_SPEC] * 9,
        out_specs=(VMEM_SPEC,) * 3,
        cost_estimate=pl.CostEstimate(flops=500_000_000, bytes_accessed=3_000_000, transcendentals=0),
        name="coarse_edge_terms",
        compiler_params=limit(16),
    )(send, edges, nodes, proj, edge_in, edge_out, node_in, node_out, bias)


def coarse_kernel(send_ref, pre_ref, own_ref, w_ref, node_ref, low_ref, high_ref, node_in, bias, gain, out_ref):
    nodes = node_ref.shape[0]
    rim = low_ref.shape[0]
    count = pre_ref.shape[0]
    rims = jnp.concatenate([low_ref[...], high_ref[...]], axis=0)
    b_message = centred_row(bias[1:2, :])
    b_update = centred_row(bias[3:4, :])
    tnodes = TILE // DEG
    collect = (
        lax.broadcasted_iota(jnp.int32, (tnodes, TILE), 1) // DEG
        == lax.broadcasted_iota(jnp.int32, (tnodes, TILE), 0)
    ).astype(F32).astype(BF16)
    picked = one_hot_rows(send_ref[...] - nodes, 2 * rim)
    hidden = jnp.maximum(pre_ref[...] + dot(picked, rims), 0.0).astype(BF16)
    m = scaled_rows(dot(hidden, w_ref[0]) + b_message).astype(BF16)
    sums = [dot(collect, m[q : q + TILE, :]) for q in range(0, count, TILE)]
    summed = (jnp.concatenate(sums, axis=0) * gain[0:1, :]).astype(BF16)
    hidden = jnp.maximum(own_ref[...] + dot(summed, node_in[1]), 0.0).astype(BF16)
    u = scaled_rows(dot(hidden, w_ref[1]) + b_update) * gain[1:2, :]
    out_ref[...] = (node_ref[...].astype(F32) + u).astype(BF16)


def coarse_level(send, terms, nodes, low, high, node_in, bias, gain):
    pre, own, w = terms
    return pl.pallas_call(
        coarse_kernel,
        out_shape=jax.ShapeDtypeStruct(nodes.shape, BF16),
        in_specs=[VMEM_SPEC] * 10,
        out_specs=VMEM_SPEC,
        cost_estimate=pl.CostEstimate(flops=500_000_000, bytes_accessed=3_000_000, transcendentals=0),
        name="coarse_level",
        compiler_params=limit(16),
    )(send, pre, own, w, nodes, low, high, node_in, bias, gain)


def pair_swaps():
    count = lax.axis_size("dom")
    inner = [(i, i ^ 1) for i in range(count)]
    outer = [(i, ((i + 1) ^ 1) - 1) for i in range(1, count - 1)]
    return inner, outer


def body(
    node_lat,
    edge_lat,
    edge_send,
    halo_list,
    pool_id,
    coarse_lat,
    cedge_lat,
    cedge_send,
    chalo_list,
    fine_edge_in,
    fine_edge_out,
    fine_node_in,
    fine_node_out,
    fine_bias,
    fine_gain,
    coarse_edge_in,
    coarse_edge_out,
    coarse_node_in,
    coarse_node_out,
    coarse_bias,
    coarse_gain,
):
    inner, outer = pair_swaps()
    odd = lax.rem(lax.axis_index("dom"), 2)
    rim = halo_list.shape[0] // 2

    def table_row(send, count, rim_rows):
        lower = jnp.where(odd == 1, count, count + rim_rows)
        upper = jnp.where(odd == 1, count + rim_rows, count)
        return jnp.where(
            send < rim_rows,
            send + lower,
            jnp.where(
                send < rim_rows + count, send - rim_rows, send - (rim_rows + count) + upper
            ),
        )

    border_b, node_near, edge_in_near = border_rows(halo_list, node_lat, fine_edge_in, rim)
    rim_b = lax.ppermute(border_b, "dom", outer)
    border_a = own_rows(halo_list, node_near, edge_in_near, rim)
    rim_a = lax.ppermute(border_a, "dom", inner)
    groups = lax.axis_size("group")
    *terms, table = edge_terms(
        edge_send.reshape(-1, 128),
        pool_id.reshape(1, -1),
        edge_lat,
        node_near,
        rim,
        edge_in_near,
        fine_edge_out,
        fine_node_in,
        fine_node_out,
        fine_bias,
    )
    fine_near, far_up, far_down = fine_level(
        terms, table, node_near, rim_a, rim_b, fine_node_in, fine_bias, fine_gain
    )
    onward = [(i, (i + 1) % groups) for i in range(groups)]
    back = [(target, source) for source, target in onward]
    far_up = lax.ppermute(far_up, "group", onward)
    far_down = lax.ppermute(far_down, "group", back)
    fine_out, next_rows, prev_rows, mine = pool_rows(pool_id.reshape(1, -1), fine_near)
    next_rows, prev_rows = relay_rows(next_rows, prev_rows, far_up, far_down)
    below = lax.ppermute(next_rows, "group", onward)
    above = lax.ppermute(prev_rows, "group", back)
    crim = chalo_list.shape[0] // 2
    clusters = coarse_lat.shape[0]
    coarse_in, coarse_proj, cborder_a, cborder_b = cluster_level(
        mine, below, above, coarse_lat, chalo_list.reshape(-1, 1), coarse_edge_in
    )
    crim_b = lax.ppermute(cborder_b, "dom", outer)
    crim_a = lax.ppermute(cborder_a, "dom", inner)
    csend = table_row(cedge_send, clusters, crim).reshape(-1, 1)
    cterms = coarse_edge_terms(
        csend,
        cedge_lat,
        coarse_in,
        coarse_proj,
        coarse_edge_in,
        coarse_edge_out,
        coarse_node_in,
        coarse_node_out,
        coarse_bias,
    )
    coarse_out = coarse_level(
        csend, cterms, coarse_in, crim_a, crim_b, coarse_node_in, coarse_bias, coarse_gain
    )
    return (fine_out, coarse_out)


def solution(mesh):
    rows = P(("group", "dom"), None)
    flat = P(("group", "dom"))
    placed = (rows, rows, flat, flat, flat, rows, rows, flat, flat) + (P(),) * 12

    return jax.shard_map(
        body,
        mesh=mesh,
        in_specs=placed,
        out_specs=(rows, rows),
        check_vma=False,
    )
```
